32 devices in a mesh: view: 4 (over z), brick: 8 (over y, x, core).
Axes of the slice: x: 2, y: 2, z: 4, core: 2. Of those that a mesh axis runs over, the one named last changes fastest.
Arguments:
- estimate: float32 [16, 16, 64, 256], P('brick'), may hold values from 0.5 to 2
- views_data: bfloat16 [4, 8, 112, 32, 128], P('view', 'brick'), may hold values from 0.5 to 2
- psf_taps: float32 [4, 3, 31], P('view'), may hold values from 0.02 to 1
- seg_owner: int32 [4, 8, 32, 1], P('view', 'brick'), may hold values from 0 to 7; in each aligned block of 32 rows (0 to 31, 32 to 63, ..., all dimensions but the last counted through in order) at most 8 rows name the same one
- seg_local: int32 [4, 8, 32], P('view', 'brick'), may hold values from 0 to 1
- seg_offset: int32 [4, 8, 32], P('view', 'brick'), may hold values from 0 to 12
- seg_extent: int32 [4, 8, 32], P('view', 'brick'), may hold values from 1 to 4, 112 in all within a row
- view_shift: int32 [4, 2], P('view'), may hold values from 0 to 32
Outputs:
- joined: float32 [16, 16, 64, 256], P('brick')
The draws below stay inside these ranges and needn't reach their ends.
Inputs may be any that keep to these rules, and one draw needn't show every extreme that they name: `seg_owner`: within one tile's 32 segments no owner is named more than 8 times, and in every draw some tile names one owner exactly 8 times. `seg_extent`: the 32 extents of a tile sum to 112, and some extent is exactly 4.
All inputs are finite; a program needn't handle non-finite values.
Results may differ from the reference program's by a relative error of at most 0.0003.
Values may be sent and summed in bfloat16 or wider, within the bound.
No kernel may reach another device: no remote copies, remote signals or barrier semaphores. Data moves between devices by JAX's collectives and lax.ppermute only.
A program may use at most 128 MiB of HBM per device.

```python
import math
import jax
import jax.numpy as jnp
import numpy as np
from jax import lax

TAPS = 31
ITERS = 2
BR_DEV = 2
BX = 16
BY = 64
BZ = 256
TY = 32
TZ = 128
EXTMAX = 4
TX = 112
SEGS = 32
CAP = 8
VIEWS = 4
READERS = 8
BRICKS = 16
N_BRICK = 8


def with_ends(entries, key, least, largest):
    place = [jax.random.randint(jax.random.fold_in(key, axis), (), 0, length) for axis, length in enumerate(entries.shape)]
    main_axis = entries.shape.index(max(entries.shape))
    beside = place[:main_axis] + [(place[main_axis] + 1) % entries.shape[main_axis]] + place[main_axis + 1:]
    return entries.at[tuple(place)].set(least).at[tuple(beside)].set(largest)


def block_scale(rng, dims, cuts, smallest, top_value):
    def one(dim, blocks):
        heights = jax.random.uniform(jax.random.fold_in(jax.random.fold_in(rng, 6), dim), (blocks,), jnp.float32, smallest / len(cuts), top_value / len(cuts))
        return jnp.repeat(jnp.exp(heights), dims[dim] // blocks).reshape((-1,) + (1,) * (len(dims) - dim - 1))

    factor_of = one(*cuts[0])
    for cut in cuts[1:]:
        factor_of = factor_of * one(*cut)
    return factor_of


def profile(amount, total, bound, skew):
    portions = [(1 << 20) // math.isqrt(standing ** skew) + 1 for standing in range(2, amount + 1)]
    rest, given = total - bound - (amount - 1), [1] * (amount - 1)
    while rest > 0:
        movable = [i for i in range(amount - 1) if given[i] < bound]
        mass, budget = sum([portions[i] for i in movable]), rest
        for i in movable:
            extra = min(bound - given[i], max(1, budget * portions[i] // mass), rest)
            given[i] = given[i] + extra
            rest = rest - extra
    return np.array([bound] + given)


def uneven(key, count, total, limit, skew):
    if count == 2:
        one = jax.random.randint(key, (), max(1, total - limit), min(limit, total - 1) + 1)
        return jnp.stack([one, total - one])
    sizes = jnp.asarray(profile(count, total, limit, skew), jnp.int32)
    twos = (count - 1) // 2
    donor, taker = sizes[1:1 + 2 * twos:2], sizes[2:2 + 2 * twos:2]
    slack = jnp.minimum(donor - 1, limit - taker)
    moved = jax.random.randint(jax.random.fold_in(key, 1), (twos,), 0, 1 << 20) % (slack + 1)
    sizes = sizes.at[1:1 + 2 * twos:2].set(donor - moved).at[2:2 + 2 * twos:2].set(taker + moved)
    return sizes[jax.random.permutation(jax.random.fold_in(key, 2), count)]


def deal_out(key, own, number, rows, amount, top, bound, slope):
    sequence = jax.random.permutation(key, amount)
    packed, ordinary = portions_of(amount, rows * top, bound, slope, True), portions_of(amount, rows * top, bound, slope, False)
    places = jnp.arange(amount)

    def named(tallies, offset_by):
        used = int((tallies > 0).sum())
        fixed = max(1, used // 4)
        shifted = fixed + (places - fixed + offset_by * (used - fixed)) % max(1, amount - fixed)
        return jnp.zeros((amount,), jnp.int32).at[sequence[jnp.where(places < fixed, places, shifted)]].set(jnp.asarray(tallies, jnp.int32))

    tallies = jnp.where(number % 4 == 0, named(packed, number // 4), named(ordinary, number - number // 4 - 1))
    mixed = jax.random.permutation(jax.random.fold_in(own, 3), amount)
    donor, taker = mixed[0:amount // 2 * 2:2], mixed[1:amount // 2 * 2:2]
    margin = jnp.minimum(tallies[donor] - 1, bound - tallies[taker]) // 2
    margin = jnp.where((donor == sequence[0]) | (taker == sequence[0]) | (tallies[taker] == 0), 0, jnp.maximum(margin, 0))
    shifted = jax.random.randint(jax.random.fold_in(own, 4), (amount // 2,), 0, 1 << 20) % (margin + 1)
    tallies = tallies.at[donor].add(-shifted).at[taker].add(shifted)
    items = jnp.searchsorted(jnp.cumsum(tallies), jnp.arange(rows * top), side="right").astype(jnp.int32)
    grid = items.reshape(top, rows).T
    grid = grid[jax.random.permutation(jax.random.fold_in(own, 1), rows)]
    offset_by = jax.random.randint(jax.random.fold_in(own, 2), (rows, 1), 0, top)
    return jnp.take_along_axis(grid, (jnp.arange(top)[None, :] + offset_by) % top, axis=1)


def portions_of(amount, total, bound, slope, full):
    portions = [(1 << 20) // math.isqrt(grade ** slope) + 1 for grade in range(1, amount + 1)]
    largest = bound if full else min(bound, max(-(-total // amount), total * portions[0] // sum(portions)))
    least = 1 if total - largest >= amount - 1 else 0
    given, spare = [largest] + [least] * (amount - 1), total - largest - least * (amount - 1)
    while spare > 0:
        movable = [i for i in range(1, amount) if given[i] < largest] or [i for i in range(1, amount) if given[i] < bound]
        whole, left = sum([portions[i] for i in movable]), spare
        for i in movable:
            addition = min(bound - given[i], max(1, left * portions[i] // whole), spare)
            given[i] = given[i] + addition
            spare = spare - addition
    return np.array(given)


def setup_inputs(seed: int = 0) -> dict:
    key_of = jax.random.split(jax.random.key(seed), 9)
    estimate = jnp.clip(0.5 + 1.5 * jax.random.uniform(key_of[0], (BRICKS, BX, BY, BZ), jnp.float32) ** block_scale(key_of[0], (BRICKS, BX, BY, BZ), ((0, 8),), -0.2, 0.2), 0.5, 2.0)
    views_data = jnp.clip(0.5 + 1.5 * jax.random.uniform(key_of[1], (VIEWS, READERS, TX, TY, TZ), jnp.float32) ** block_scale(key_of[1], (VIEWS, READERS, TX, TY, TZ), ((0, 4), (1, 8)), -0.2, 0.2), 0.5, 2.0).astype(jnp.bfloat16)
    psf_taps = jnp.clip(jnp.exp(math.log(1.0) - 3.912023 * jax.random.uniform(key_of[2], (VIEWS, 3, TAPS), jnp.float32) ** block_scale(key_of[2], (VIEWS, 3, TAPS), ((0, 4),), -0.2, 0.2)), 0.02, 1.0)
    seg_owner_keys = jax.random.split(jax.random.fold_in(key_of[3], 1), VIEWS * READERS * SEGS // SEGS)
    seg_owner_turns = jax.random.permutation(jax.random.fold_in(key_of[3], 3), VIEWS * READERS * SEGS // SEGS)
    seg_owner = jax.vmap(lambda own, number: deal_out(jax.random.fold_in(key_of[3], 2), own, number, SEGS, N_BRICK, 1, CAP, 2))(seg_owner_keys, seg_owner_turns).reshape((VIEWS, READERS, SEGS, 1))
    seg_local = with_ends(jax.random.randint(key_of[4], (VIEWS, READERS, SEGS), 0, BR_DEV), jax.random.fold_in(key_of[4], 1), 0, BR_DEV - 1).astype(jnp.int32)
    seg_offset = with_ends(jax.random.randint(key_of[5], (VIEWS, READERS, SEGS), 0, BX - EXTMAX + 1), jax.random.fold_in(key_of[5], 1), 0, BX - EXTMAX).astype(jnp.int32)
    seg_extent = jax.vmap(lambda own: uneven(own, SEGS, TX, EXTMAX, 1))(jax.random.split(key_of[6], VIEWS * READERS)).reshape((VIEWS, READERS, SEGS)).astype(jnp.int32)
    view_shift = with_ends(jax.random.randint(key_of[7], (VIEWS, 2), 0, min(BY - TY, BZ - TZ) + 1), jax.random.fold_in(key_of[7], 1), 0, min(BY - TY, BZ - TZ)).astype(jnp.int32)
    return {"estimate": estimate, "views_data": views_data, "psf_taps": psf_taps, "seg_owner": seg_owner, "seg_local": seg_local, "seg_offset": seg_offset, "seg_extent": seg_extent, "view_shift": view_shift}


def blur_matrix(tap_values, length):
    centre = tap_values.shape[0] // 2
    positions = jnp.arange(length, dtype=jnp.int32)
    offsets_tab = positions[:, None] - positions[None, :] + centre
    match_table = (offsets_tab[:, :, None] == jnp.arange(tap_values.shape[0], dtype=jnp.int32)[None, None, :]).astype(tap_values.dtype)
    return jnp.sum(match_table * tap_values[None, None, :], axis=-1)


def apply_blur(volume, matrices):
    along_z, along_y, along_x = matrices
    highest = lax.Precision.HIGHEST
    volume = jnp.einsum("...xyz,zw->...xyw", volume, along_z, precision=highest)
    volume = jnp.einsum("...xyz,yw->...xwz", volume, along_y, precision=highest)
    volume = jnp.einsum("...xyz,xw->...wyz", volume, along_x, precision=highest)
    return volume


def view_matrices(view_taps, tile_x, tile_y, tile_z):
    normed = view_taps / jnp.sum(view_taps, axis=1, keepdims=True)
    forward = (blur_matrix(normed[2], tile_z), blur_matrix(normed[1], tile_y), blur_matrix(normed[0], tile_x))
    backward = (forward[0].T, forward[1].T, forward[2].T)
    return forward, backward


def source_rows(owners, local_ids, offsets, extents, tile_x, brick_x, per_owner):
    starts = (jnp.cumsum(extents, axis=1) - extents).astype(jnp.int32)
    tile_rows = jnp.arange(tile_x, dtype=jnp.int32)
    seg_of = (jnp.sum((starts[:, None, :] <= tile_rows[None, :, None]).astype(jnp.int32), axis=2) - 1).astype(jnp.int32)

    def select_rows(values):
        return jnp.take_along_axis(values, seg_of, axis=1)

    brick_ids = select_rows(owners) * per_owner + select_rows(local_ids)
    return (brick_ids * brick_x + select_rows(offsets) + tile_rows[None, :] - select_rows(starts)).astype(jnp.int32)


def reference(estimate, views_data, psf_taps, seg_owner, seg_local, seg_offset, seg_extent, view_shift):
    bricks, brick_x, brick_y, brick_z = estimate.shape
    view_count, readers, tile_x, tile_y, tile_z = views_data.shape
    per_owner = bricks // readers
    all_rows = bricks * brick_x
    geometry = []
    weight = jnp.zeros((all_rows, brick_y, brick_z), jnp.float32)
    for view_idx in range(view_count):
        forward, backward = view_matrices(psf_taps[view_idx], tile_x, tile_y, tile_z)
        source = source_rows(seg_owner[view_idx, :, :, 0], seg_local[view_idx], seg_offset[view_idx], seg_extent[view_idx], tile_x, brick_x, per_owner).reshape(-1)
        shift_y = view_shift[view_idx, 0].astype(jnp.int32)
        shift_z = view_shift[view_idx, 1].astype(jnp.int32)
        ones_back = apply_blur(jnp.ones((tile_x, tile_y, tile_z), jnp.float32), backward)
        placed = jnp.zeros((all_rows, tile_y, tile_z), jnp.float32).at[source].add(jnp.tile(ones_back, (readers, 1, 1)))
        weight = weight + lax.dynamic_update_slice(jnp.zeros((all_rows, brick_y, brick_z), jnp.float32), placed, (jnp.int32(0), shift_y, shift_z))
        geometry.append((forward, backward, source, shift_y, shift_z))
    flat_est = estimate.reshape(all_rows, brick_y, brick_z)
    for sweep in range(ITERS):
        correction = jnp.zeros((all_rows, brick_y, brick_z), jnp.float32)
        for view_idx in range(view_count):
            forward, backward, source, shift_y, shift_z = geometry[view_idx]
            cropped = lax.dynamic_slice(flat_est, (jnp.int32(0), shift_y, shift_z), (all_rows, tile_y, tile_z))
            view_tile = lax.optimization_barrier(cropped[source].astype(jnp.bfloat16)).astype(jnp.float32)
            view_tile = view_tile.reshape(readers, tile_x, tile_y, tile_z)
            blurred = apply_blur(view_tile, forward)
            quotient = views_data[view_idx].astype(jnp.float32) / blurred
            projected = apply_blur(quotient, backward).reshape(-1, tile_y, tile_z)
            placed = jnp.zeros((all_rows, tile_y, tile_z), jnp.float32).at[source].add(projected)
            correction = correction + lax.dynamic_update_slice(jnp.zeros((all_rows, brick_y, brick_z), jnp.float32), placed, (jnp.int32(0), shift_y, shift_z))
        flat_est = flat_est * (1.0 + correction) / (1.0 + weight)
    return flat_est.reshape(bricks, brick_x, brick_y, brick_z)
```

```python
import jax
import jax.numpy as jnp
from jax import lax
from jax.experimental import pallas as pl
from jax.experimental.pallas import tpu as pltpu
from jax.sharding import PartitionSpec as P

ITERS = 2
WIRE = jnp.float32
F32 = jnp.float32
BF16 = jnp.bfloat16


def split(x):
    hi = x.astype(BF16)
    return hi, (x - hi.astype(F32)).astype(BF16)


def split_outside(x):
    hi = lax.reduce_precision(x, 8, 7)
    return hi.astype(BF16), lax.reduce_precision(x - hi, 8, 7).astype(BF16)


def dot(a, b):
    return lax.dot_general(a, b, (((1,), (0,)), ((), ())), preferred_element_type=F32)


def band(taps, rows, cols):
    count = taps.shape[0]
    index = rows[:, None] - cols[None, :] + count // 2
    hit = index[:, :, None] == jnp.arange(count, dtype=jnp.int32)
    return jnp.sum(jnp.where(hit, taps, 0.0), axis=-1)


def crop_rows(value, shift_y, shift_z, tile_y, tile_z, stage):
    brick_z = value.shape[1]
    turned = pltpu.roll(value, lax.rem(brick_z - shift_z, brick_z), 1)
    stage[...] = turned[:, :tile_z]
    return stage[pl.ds(shift_y, tile_y), :]


def first_crop(shifts, estimate, tile_y, tile_z):
    rows, brick_y, brick_z = estimate.shape

    def kernel(shift_ref, est_ref, out_ref, stage, crops):
        def step(r, carry):
            crops[pl.ds(r, tile_y, stride=rows), :] = crop_rows(
                est_ref[r], shift_ref[0], shift_ref[1], tile_y, tile_z, stage
            )
            return carry

        lax.fori_loop(0, rows, step, 0, unroll=4)
        out_ref[...] = crops[...].astype(BF16).reshape(tile_y, rows, tile_z)

    return pl.pallas_call(
        kernel,
        out_shape=jax.ShapeDtypeStruct((tile_y, rows, tile_z), BF16),
        in_specs=[
            pl.BlockSpec(memory_space=pltpu.SMEM),
            pl.BlockSpec(memory_space=pltpu.VMEM),
        ],
        out_specs=pl.BlockSpec(memory_space=pltpu.VMEM),
        scratch_shapes=[
            pltpu.VMEM((brick_y, tile_z), F32),
            pltpu.VMEM((tile_y * rows, tile_z), F32),
        ],
        name="first_crop",
    )(shifts, estimate)


def read_tile(pieces, measured, gather_mat, scatter_mat, z_mat, y_mat, slots, with_weight):
    owners = len(pieces)
    half, rows, tile_z = pieces[0][0].shape
    tile_y = 2 * half
    tile_x = measured.shape[0] // tile_y
    flat = [p for pair in pieces for p in pair]
    n_send = owners // 2
    group = y_mat.shape[1] // 2
    per_group = group // tile_y
    groups = tile_x // per_group
    extra = (1 if with_weight else 0, 0)

    def kernel(*refs):
        g_refs = refs[: 2 * owners]
        m_ref, gm_ref, sm_ref, zm_ref, ym_ref = refs[2 * owners : 2 * owners + 5]
        outs = refs[2 * owners + 5 : 2 * owners + 9]
        buf = refs[2 * owners + 9]
        for h in range(2):
            parts = [g_refs[2 * k + h] for k in range(owners)]

            def gather(i, carry):
                y = i * 2
                both = jnp.concatenate(
                    [
                        jnp.concatenate([p[y], p[y + 1]], axis=1)
                        for p in parts
                    ],
                    axis=0,
                )
                got = dot(gm_ref[...], both)
                got = got[:tile_x] + got[tile_x:]
                stacked = jnp.concatenate([got[:, :tile_z], got[:, tile_z:]], axis=0)
                hi, lo = split(stacked)
                out = dot(jnp.concatenate([hi, lo], axis=1), zm_ref[...])
                out = out[:, :tile_z] + out[:, tile_z:]
                buf[pl.ds(h * half + y, tile_x, stride=tile_y), :] = out[:tile_x]
                buf[pl.ds(h * half + y + 1, tile_x, stride=tile_y), :] = out[tile_x:]
                return carry

            lax.fori_loop(0, half // 2, gather, 0, unroll=2)

        def divide(i, carry):
            at = pl.multiple_of(i * 2 * group, 2 * group)
            first = buf[pl.ds(at, group), :]
            second = buf[pl.ds(at + group, group), :]
            hi, lo = split(jnp.concatenate([first, second], axis=1))
            out = dot(ym_ref[...], jnp.concatenate([hi, lo], axis=0))
            out = out[:group] + out[group:]
            data = m_ref[pl.ds(at, 2 * group), :].astype(F32)
            buf[pl.ds(at, group), :] = data[:group] / out[:, :tile_z]
            buf[pl.ds(at + group, group), :] = data[group:] / out[:, tile_z:]
            return carry

        lax.fori_loop(0, groups // 2, divide, 0, unroll=2)

        for h in range(2):
            send_ref, keep_ref = outs[2 * h], outs[2 * h + 1]

            def put(y, sums, send_ref=send_ref, keep_ref=keep_ref, h=h):
                for k in range(owners):
                    block = sums[k * rows : (k + 1) * rows]
                    slot = slots[h][k]
                    if slot < n_send:
                        send_ref[slot, y] = block.astype(send_ref.dtype)
                    else:
                        keep_ref[slot - n_send, y] = block

            def scatter(i, carry, h=h, put=put):
                y = i * 2
                first = buf[pl.ds(h * half + y, tile_x, stride=tile_y), :]
                second = buf[pl.ds(h * half + y + 1, tile_x, stride=tile_y), :]
                hi, lo = split(jnp.concatenate([first, second], axis=1))
                out = dot(sm_ref[...], jnp.concatenate([hi, lo], axis=0))
                out = out[: owners * rows] + out[owners * rows :]
                put(y, out[:, :tile_z])
                put(y + 1, out[:, tile_z:])
                return carry

            lax.fori_loop(0, half // 2, scatter, 0, unroll=2)
            if extra[h]:
                ones = jnp.ones((tile_x, tile_z), BF16)
                out = dot(sm_ref[:, :tile_x], ones)
                put(half, out[: owners * rows] + out[owners * rows :])

    vmem = pl.BlockSpec(memory_space=pltpu.VMEM)
    shapes = []
    for h in range(2):
        for dtype in (WIRE, F32):
            shapes.append(jax.ShapeDtypeStruct((n_send, half + extra[h], rows, tile_z), dtype))
    return pl.pallas_call(
        kernel,
        out_shape=tuple(shapes),
        in_specs=[vmem] * (2 * owners + 5),
        out_specs=(vmem,) * 4,
        scratch_shapes=[pltpu.VMEM((tile_x * tile_y, tile_z), F32)],
        name="read_tile",
    )(*flat, measured, gather_mat, scatter_mat, z_mat, y_mat)


def update(scalars, sums, estimate, z_place, y_place, outline, row_weight, tile_y, tile_z, last):
    views = len(sums)
    rows, brick_y, brick_z = estimate.shape
    half = tile_y // 2
    flat = [p for pair in sums for p in pair]

    def kernel(*refs):
        s_ref = refs[0]
        in_refs = refs[1 : 1 + 2 * views]
        est_ref, zp_ref, yp_ref, pat_ref, rw_ref = refs[1 + 2 * views : 6 + 2 * views]
        rest = refs[6 + 2 * views :]
        out_ref = rest[0]
        crop_ref = None if last else rest[1]
        placed, stage, crops = rest[-3:]
        me = s_ref[2]
        for s in range(views):
            view = lax.rem(me + views - s, views)
            for h in range(2):
                src = in_refs[2 * s + h]
                x = src[pl.ds(0, half)].astype(F32).reshape(half * rows, tile_z)
                hi, lo = split(x)
                out = dot(jnp.concatenate([hi, lo], axis=1), zp_ref[view, 0])
                out = out + dot(hi, zp_ref[view, 1, :tile_z, :])
                at = pl.multiple_of((view * 2 + h) * half * rows, half * rows)
                for j in range(brick_z // tile_z):
                    placed[j, pl.ds(at, half * rows), :] = out[:, j * tile_z : (j + 1) * tile_z]

        def step(r, carry):
            x = jnp.concatenate(
                [
                    placed[j, pl.ds(r, views * tile_y, stride=rows), :]
                    for j in range(brick_z // tile_z)
                ],
                axis=1,
            )
            hi, lo = split(x)
            out = dot(yp_ref[...], jnp.concatenate([hi, lo], axis=0))
            correction = out[:brick_y] + out[brick_y:]
            weight = jnp.zeros((brick_y, brick_z), F32)
            for v in range(views):
                factor = rw_ref[v, pl.ds(r, 1), :]
                factor = jnp.concatenate([factor] * (brick_z // factor.shape[1]), axis=1)
                weight = weight + factor * pat_ref[v]
            value = est_ref[r] * (1.0 + correction) / (1.0 + weight)
            out_ref[r] = value
            if not last:
                crops[pl.ds(r, tile_y, stride=rows), :] = crop_rows(
                    value, s_ref[0], s_ref[1], tile_y, tile_z, stage
                )
            return carry

        lax.fori_loop(0, rows, step, 0, unroll=2)
        if not last:
            crop_ref[...] = crops[...].astype(BF16).reshape(tile_y, rows, tile_z)

    vmem = pl.BlockSpec(memory_space=pltpu.VMEM)
    shapes = [jax.ShapeDtypeStruct(estimate.shape, F32)]
    if not last:
        shapes.append(jax.ShapeDtypeStruct((tile_y, rows, tile_z), BF16))
    return pl.pallas_call(
        kernel,
        out_shape=tuple(shapes),
        in_specs=[pl.BlockSpec(memory_space=pltpu.SMEM)] + [vmem] * (2 * views + 5),
        out_specs=(vmem,) * len(shapes),
        scratch_shapes=[
            pltpu.VMEM((brick_z // tile_z, views * tile_y * rows, tile_z), F32),
            pltpu.VMEM((brick_y, tile_z), F32),
            pltpu.VMEM((tile_y * rows, tile_z), F32),
        ],
        name="update",
    )(scalars, *flat, estimate, z_place, y_place, outline, row_weight)


def flip(x, bit, count):
    return lax.ppermute(x, "brick", [(i, i ^ bit) for i in range(count)])


def gather_owners(crop, count):
    half = crop.shape[0] // 2
    got = {0: (crop[:half], crop[half:])}
    bits = [1 << i for i in range(count.bit_length() - 1)]
    wide = bits[1:]
    if len(wide) == 2:
        x, y = wide
        over_x = flip(crop, x, count)
        over_y = flip(crop, y, count)
        got[x] = (over_x[:half], over_x[half:])
        got[y] = (over_y[:half], over_y[half:])
        got[x | y] = (flip(over_x[:half], y, count), flip(over_y[half:], x, count))
        core = {0: flip(crop, 1, count), x: flip(over_x, 1, count), y: flip(over_y, 1, count)}
        for k, value in core.items():
            got[k | 1] = (value[:half], value[half:])
        got[x | y | 1] = tuple(flip(p, 1, count) for p in got[x | y])
    else:
        for bit in wide + [1]:
            for k in list(got):
                got[k ^ bit] = tuple(flip(p, bit, count) for p in got[k])
    return [got[k] for k in range(count)]


def halving_orders(count):
    bits = [1 << i for i in range(count.bit_length() - 1)]
    orders = [bits, bits[:1] + bits[:0:-1]]
    slots = []
    for order in orders:
        place = {}
        for k in range(count):
            slot = 0
            for bit in order:
                slot = slot * 2 + (0 if k & bit else 1)
            place[k] = slot
        slots.append(place)
    return orders, slots


def on_device(
    estimate, views_data, psf_taps, seg_owner, seg_local, seg_offset, seg_extent, view_shift
):
    per_owner, brick_x, brick_y, brick_z = estimate.shape
    tile_x, tile_y, tile_z = views_data.shape[2:]
    own_rows = per_owner * brick_x
    owners = lax.axis_size("brick")
    views = lax.axis_size("view")
    me = lax.axis_index("brick")
    my_view = lax.axis_index("view")
    half = tile_y // 2
    highest = lax.Precision.HIGHEST

    flat = estimate.reshape(own_rows, brick_y, brick_z)
    shifts = view_shift[0]
    scalars = jnp.concatenate([shifts, my_view[None].astype(jnp.int32)])
    crop = first_crop(scalars, flat, tile_y, tile_z)

    taps = psf_taps[0] / jnp.sum(psf_taps[0], axis=1, keepdims=True)
    count = taps.shape[1]
    lanes = 128
    meta = jnp.zeros((8, lanes), F32)
    meta = meta.at[0, :count].set(taps[1]).at[1, :count].set(taps[2])
    meta = meta.at[2, :2].set(shifts.astype(F32))
    around = [meta] + [
        lax.ppermute(meta, "view", [(i, (i + s) % views) for i in range(views)])
        for s in range(1, views)
    ]
    view_ids = jnp.arange(views, dtype=jnp.int32)
    steps_back = lax.rem(my_view - view_ids + views, views)
    metas = sum(
        jnp.where((steps_back == s)[:, None, None], around[s][None], 0.0) for s in range(views)
    )
    all_shifts = metas[:, 2, :2].astype(jnp.int32)

    tile_rows = jnp.arange(tile_x, dtype=jnp.int32)
    tile_cols = jnp.arange(tile_z, dtype=jnp.int32)
    tile_mids = jnp.arange(tile_y, dtype=jnp.int32)
    extent = seg_extent[0, 0]
    seg_ids = jnp.arange(extent.shape[0], dtype=jnp.int32)
    starts = jnp.sum(jnp.where(seg_ids[None, :] < seg_ids[:, None], extent[None, :], 0), axis=1)
    base = (
        (seg_owner[0, 0, :, 0] ^ me) * own_rows + seg_local[0, 0] * brick_x + seg_offset[0, 0]
    )
    inside = (starts[None, :] <= tile_rows[:, None]) & (
        tile_rows[:, None] < (starts + extent)[None, :]
    )
    source = jnp.sum(jnp.where(inside, (base - starts)[None, :], 0), axis=1) + tile_rows
    picks = (
        source[:, None] == jnp.arange(owners * own_rows, dtype=jnp.int32)[None, :]
    ).astype(F32)
    x_mat = band(taps[0], tile_rows, tile_rows)
    rows_mat = jnp.einsum("tw,tr->wr", x_mat, picks, precision=highest)
    hi, lo = split_outside(rows_mat)
    gather_mat = jnp.concatenate([hi, lo], axis=0)
    scatter_mat = jnp.concatenate(
        [jnp.concatenate([hi.T, hi.T], axis=1), jnp.concatenate([lo.T, lo.T], axis=1)], axis=0
    )
    hi, lo = split_outside(band(taps[2], tile_cols, tile_cols))
    pair = jnp.concatenate([hi, lo], axis=1)
    z_mat = jnp.concatenate([pair, pair], axis=0)
    per_group = max(1, 128 // tile_y)
    y_mat = jnp.kron(
        jnp.eye(per_group, dtype=F32), band(taps[1], tile_mids, tile_mids).T
    )
    hi, lo = split_outside(y_mat)
    y_mat = jnp.concatenate(
        [jnp.concatenate([hi, hi], axis=1), jnp.concatenate([lo, lo], axis=1)], axis=0
    )

    def placing(values, shift, long, short):
        at = jnp.arange(long, dtype=jnp.int32) - shift
        mat = band(values, at, jnp.arange(short, dtype=jnp.int32))
        return jnp.where(((at >= 0) & (at < short))[:, None], mat, 0.0)

    z_all = jax.vmap(lambda m, s: placing(m[1, :count], s[1], brick_z, tile_z).T)(
        metas, all_shifts
    )
    y_all = jax.vmap(lambda m, s: placing(m[0, :count], s[0], brick_y, tile_y))(
        metas, all_shifts
    )
    outline = jnp.sum(y_all, axis=2)[:, :, None] * jnp.sum(z_all, axis=1)[:, None, :]
    hi, lo = split_outside(z_all)
    z_place = jnp.stack(
        [jnp.concatenate([hi, hi], axis=1), jnp.concatenate([lo, lo], axis=1)], axis=1
    )
    y_wide = jnp.transpose(y_all, (1, 0, 2)).reshape(brick_y, views * tile_y)
    hi, lo = split_outside(y_wide)
    y_place = jnp.concatenate(
        [jnp.concatenate([hi, hi], axis=1), jnp.concatenate([lo, lo], axis=1)], axis=0
    )
    measured = views_data.reshape(tile_x * tile_y, tile_z)
    orders, slots = halving_orders(owners)

    row_weight = None
    current = flat
    for sweep in range(ITERS):
        last = sweep == ITERS - 1
        pieces = gather_owners(crop, owners)
        outs = read_tile(
            pieces, measured, gather_mat, scatter_mat, z_mat, y_mat, slots, sweep == 0
        )
        send = [outs[0], outs[2]]
        keep = [outs[1], outs[3]]
        for i in range(len(orders[0])):
            for h in range(2):
                total = keep[h] + flip(send[h], orders[h][i], owners).astype(F32)
                left = total.shape[0] // 2
                send[h] = total[:left].astype(WIRE) if left else None
                keep[h] = total[left:]
        mine = [k[0].astype(WIRE) for k in keep]
        sums = [tuple(mine)] + [
            tuple(
                lax.ppermute(p, "view", [(i, (i + s) % views) for i in range(views)])
                for p in mine
            )
            for s in range(1, views)
        ]
        if sweep == 0:
            row_weight = sum(
                jnp.where((steps_back == s)[:, None, None], sums[s][0][half][None], 0.0)
                for s in range(views)
            )
        result = update(
            scalars, sums, current, z_place, y_place, outline, row_weight, tile_y, tile_z, last
        )
        current = result[0]
        if not last:
            crop = result[1]
    return current.reshape(estimate.shape)


def solution(mesh):
    placed = (
        P("brick", None, None, None),
        P("view", "brick", None, None, None),
        P("view", None, None),
        P("view", "brick", None, None),
        P("view", "brick", None),
        P("view", "brick", None),
        P("view", "brick", None),
        P("view", None),
    )
    return jax.shard_map(
        on_device,
        mesh=mesh,
        in_specs=placed,
        out_specs=P("brick", None, None, None),
        check_vma=False,
    )
```

```python
import jax
import jax.numpy as jnp
from jax import lax
from jax.experimental import pallas as pl
from jax.experimental.pallas import tpu as pltpu
from jax.sharding import PartitionSpec as P

ITERS = 2
WIRE = jnp.int16
FULL = 32000.0
F32 = jnp.float32
BF16 = jnp.bfloat16


def split(x):
    hi = x.astype(BF16)
    return hi, (x - hi.astype(F32)).astype(BF16)


def split_outside(x):
    hi = lax.reduce_precision(x, 8, 7)
    return hi.astype(BF16), lax.reduce_precision(x - hi, 8, 7).astype(BF16)


def dot(a, b):
    return lax.dot_general(a, b, (((1,), (0,)), ((), ())), preferred_element_type=F32)


def band(taps, rows, cols):
    count = taps.shape[0]
    index = rows[:, None] - cols[None, :] + count // 2
    hit = index[:, :, None] == jnp.arange(count, dtype=jnp.int32)
    return jnp.sum(jnp.where(hit, taps, 0.0), axis=-1)


def crop_rows(ref, r, shift_y, shift_z, tile_y, tile_z, stage):
    brick_y, brick_z = ref.shape[1:]
    base = pl.multiple_of(jnp.minimum(shift_y // 8, (brick_y - tile_y) // 8 - 1) * 8, 8)
    value = ref[r, pl.ds(base, tile_y + 8), :]
    stage[...] = pltpu.roll(value, lax.rem(brick_z - shift_z, brick_z), 1)[:, :tile_z]
    return stage[pl.ds(shift_y - base, tile_y), :]


def first_crop(shifts, estimate, tile_y, tile_z):
    rows, brick_y, brick_z = estimate.shape

    def kernel(shift_ref, est_ref, out_ref, stage, crops):
        def step(r, carry):
            crops[pl.ds(r, tile_y, stride=rows), :] = crop_rows(
                est_ref, r, shift_ref[0, 0], shift_ref[0, 1], tile_y, tile_z, stage
            )
            return carry

        lax.fori_loop(0, rows, step, 0, unroll=4)
        out_ref[...] = crops[...].astype(BF16).reshape(tile_y, rows, tile_z)

    return pl.pallas_call(
        kernel,
        out_shape=jax.ShapeDtypeStruct((tile_y, rows, tile_z), BF16),
        in_specs=[
            pl.BlockSpec(memory_space=pltpu.SMEM),
            pl.BlockSpec(memory_space=pltpu.VMEM),
        ],
        out_specs=pl.BlockSpec(memory_space=pltpu.VMEM),
        scratch_shapes=[
            pltpu.VMEM((tile_y + 8, tile_z), F32),
            pltpu.VMEM((tile_y * rows, tile_z), F32),
        ],
        name="first_crop",
    )(shifts, estimate)


def code(x):
    return (x + 0.5).astype(jnp.int32).astype(WIRE)


def read_tile(pieces, measured, pattern, gather_mat, scatter_mat, z_mat, y_mat, slots):
    owners = len(pieces)
    rows, tile_z = pieces[0][0].shape[1:]
    tile_y = sum(p.shape[0] for p in pieces[0])
    half = tile_y // 2
    tile_x = measured.shape[0] // tile_y
    flat = [p for parts in pieces for p in parts]
    n_flat = len(flat)
    firsts = [sum(len(p) for p in pieces[:k]) for k in range(owners)]
    n_send = owners // 2
    group = y_mat.shape[1] // 2
    per_group = group // tile_y
    groups = tile_x // per_group

    def kernel(*refs):
        g_refs = refs[:n_flat]
        m_ref, pat_ref, gm_ref, sm_ref, zm_ref, ym_ref = refs[n_flat : n_flat + 6]
        outs = refs[n_flat + 6 : n_flat + 10]
        buf = refs[n_flat + 10]
        for h in range(2):

            def line(k, y, h=h):
                if len(pieces[k]) == 2:
                    return g_refs[firsts[k] + h][y]
                return g_refs[firsts[k]][h * half + y]

            def gather(i, carry, h=h, line=line):
                y = i * 2
                both = jnp.concatenate(
                    [
                        jnp.concatenate([line(k, y), line(k, y + 1)], axis=1)
                        for k in range(owners)
                    ],
                    axis=0,
                )
                got = dot(gm_ref[...], both)
                got = got[:tile_x] + got[tile_x:]
                stacked = jnp.concatenate([got[:, :tile_z], got[:, tile_z:]], axis=0)
                hi, lo = split(stacked)
                out = dot(jnp.concatenate([hi, lo], axis=1), zm_ref[...])
                out = out[:, :tile_z] + out[:, tile_z:]
                buf[pl.ds(h * half + y, tile_x, stride=tile_y), :] = out[:tile_x]
                buf[pl.ds(h * half + y + 1, tile_x, stride=tile_y), :] = out[tile_x:]
                return carry

            lax.fori_loop(0, half // 2, gather, 0, unroll=2)

        def divide(i, carry):
            at = pl.multiple_of(i * 2 * group, 2 * group)
            first = buf[pl.ds(at, group), :]
            second = buf[pl.ds(at + group, group), :]
            hi, lo = split(jnp.concatenate([first, second], axis=1))
            out = dot(ym_ref[...], jnp.concatenate([hi, lo], axis=0))
            out = out[:group] + out[group:]
            data = m_ref[pl.ds(at, 2 * group), :].astype(F32)
            pat = pat_ref[...]
            buf[pl.ds(at, group), :] = data[:group] * pat / out[:, :tile_z]
            buf[pl.ds(at + group, group), :] = data[group:] * pat / out[:, tile_z:]
            return carry

        lax.fori_loop(0, groups // 2, divide, 0, unroll=2)

        for h in range(2):
            send_ref, keep_ref = outs[2 * h], outs[2 * h + 1]

            def put(y, sums, send_ref=send_ref, keep_ref=keep_ref, h=h):
                for k in range(owners):
                    block = sums[k * rows : (k + 1) * rows]
                    slot = slots[h][k]
                    if slot < n_send:
                        send_ref[slot, y] = code(block)
                    else:
                        keep_ref[slot - n_send, y] = block

            def scatter(i, carry, h=h, put=put):
                y = i * 2
                first = buf[pl.ds(h * half + y, tile_x, stride=tile_y), :]
                second = buf[pl.ds(h * half + y + 1, tile_x, stride=tile_y), :]
                hi, lo = split(jnp.concatenate([first, second], axis=1))
                out = dot(sm_ref[...], jnp.concatenate([hi, lo], axis=0))
                out = out[: owners * rows] + out[owners * rows :]
                put(y, out[:, :tile_z])
                put(y + 1, out[:, tile_z:])
                return carry

            lax.fori_loop(0, half // 2, scatter, 0, unroll=2)

    vmem = pl.BlockSpec(memory_space=pltpu.VMEM)
    shapes = []
    for h in range(2):
        for dtype in (WIRE, F32):
            shapes.append(jax.ShapeDtypeStruct((n_send, half, rows, tile_z), dtype))
    return pl.pallas_call(
        kernel,
        out_shape=tuple(shapes),
        in_specs=[vmem] * (n_flat + 6),
        out_specs=(vmem,) * 4,
        scratch_shapes=[pltpu.VMEM((tile_x * tile_y, tile_z), F32)],
        name="read_tile",
    )(*flat, measured, pattern, gather_mat, scatter_mat, z_mat, y_mat)


def update(
    scalars, sums, estimate, unit, z_place, y_place, outline, row_weight, tile_y, tile_z, last
):
    views = len(sums)
    rows, brick_y, brick_z = estimate.shape
    half = tile_y // 2
    flat = [p for pair in sums for p in pair]

    def kernel(*refs):
        s_ref = refs[0]
        in_refs = refs[1 : 1 + 2 * views]
        est_ref, un_ref, zp_ref, yp_ref, pat_ref, rw_ref = refs[1 + 2 * views : 7 + 2 * views]
        rest = refs[7 + 2 * views :]
        out_ref = rest[0]
        crop_ref = None if last else rest[1]
        placed, stage, crops = rest[-3:]
        me = s_ref[2]
        for s in range(views):
            view = lax.rem(me + views - s, views)
            for h in range(2):
                src = in_refs[2 * s + h]
                x = src[...].astype(jnp.int32).astype(F32) * un_ref[view][None]
                x = x.reshape(half * rows, tile_z)
                hi, lo = split(x)
                out = dot(jnp.concatenate([hi, lo], axis=1), zp_ref[view, 0])
                out = out + dot(hi, zp_ref[view, 1, :tile_z, :])
                at = pl.multiple_of((view * 2 + h) * half * rows, half * rows)
                for j in range(brick_z // tile_z):
                    placed[j, pl.ds(at, half * rows), :] = out[:, j * tile_z : (j + 1) * tile_z]

        def step(r, carry):
            x = jnp.concatenate(
                [
                    placed[j, pl.ds(r, views * tile_y, stride=rows), :]
                    for j in range(brick_z // tile_z)
                ],
                axis=1,
            )
            hi, lo = split(x)
            out = dot(yp_ref[...], jnp.concatenate([hi, lo], axis=0))
            correction = out[:brick_y] + out[brick_y:]
            weight = jnp.zeros((brick_y, brick_z), F32)
            for v in range(views):
                factor = rw_ref[v, pl.ds(r, 1), :]
                factor = jnp.concatenate([factor] * (brick_z // factor.shape[1]), axis=1)
                weight = weight + factor * pat_ref[v]
            value = est_ref[r] * (1.0 + correction) / (1.0 + weight)
            out_ref[r] = value
            if not last:
                crops[pl.ds(r, tile_y, stride=rows), :] = crop_rows(
                    out_ref, r, s_ref[0], s_ref[1], tile_y, tile_z, stage
                )
            return carry

        lax.fori_loop(0, rows, step, 0, unroll=2)
        if not last:
            crop_ref[...] = crops[...].astype(BF16).reshape(tile_y, rows, tile_z)

    vmem = pl.BlockSpec(memory_space=pltpu.VMEM)
    shapes = [jax.ShapeDtypeStruct(estimate.shape, F32)]
    if not last:
        shapes.append(jax.ShapeDtypeStruct((tile_y, rows, tile_z), BF16))
    return pl.pallas_call(
        kernel,
        out_shape=tuple(shapes),
        in_specs=[pl.BlockSpec(memory_space=pltpu.SMEM)] + [vmem] * (2 * views + 6),
        out_specs=(vmem,) * len(shapes),
        scratch_shapes=[
            pltpu.VMEM((brick_z // tile_z, views * tile_y * rows, tile_z), F32),
            pltpu.VMEM((tile_y + 8, tile_z), F32),
            pltpu.VMEM((tile_y * rows, tile_z), F32),
        ],
        name="update",
    )(scalars, *flat, estimate, unit, z_place, y_place, outline, row_weight)


def flip(x, bit, count):
    return lax.ppermute(x, "brick", [(i, i ^ bit) for i in range(count)])


def gather_owners(crop, count):
    half = crop.shape[0] // 2
    bits = [1 << i for i in range(count.bit_length() - 1)]
    wide = bits[1:]
    got = {0: (crop,)}
    if len(wide) == 2:
        x, y = wide
        got[x] = (flip(crop, x, count),)
        got[y] = (flip(crop, y, count),)
        got[x | y] = (flip(got[x][0][:half], y, count), flip(got[y][0][half:], x, count))
        wide = []
    for bit in wide + [1]:
        for k in list(got):
            got[k ^ bit] = tuple(flip(p, bit, count) for p in got[k])
    return [got[k] for k in range(count)]


def halving_orders(count):
    bits = [1 << i for i in range(count.bit_length() - 1)]
    orders = [bits, bits[:1] + bits[:0:-1]]
    slots = []
    for order in orders:
        place = {}
        for k in range(count):
            slot = 0
            for bit in order:
                slot = slot * 2 + (0 if k & bit else 1)
            place[k] = slot
        slots.append(place)
    return orders, slots


def on_device(
    estimate, views_data, psf_taps, seg_owner, seg_local, seg_offset, seg_extent, view_shift
):
    per_owner, brick_x, brick_y, brick_z = estimate.shape
    tile_x, tile_y, tile_z = views_data.shape[2:]
    own_rows = per_owner * brick_x
    owners = lax.axis_size("brick")
    views = lax.axis_size("view")
    me = lax.axis_index("brick")
    my_view = lax.axis_index("view")
    highest = lax.Precision.HIGHEST

    flat = estimate.reshape(own_rows, brick_y, brick_z)
    crop = first_crop(view_shift, flat, tile_y, tile_z)
    shifts = view_shift[0]
    scalars = jnp.concatenate([shifts, my_view[None].astype(jnp.int32)])

    taps = psf_taps[0] / jnp.sum(psf_taps[0], axis=1, keepdims=True)
    count = taps.shape[1]
    tile_rows = jnp.arange(tile_x, dtype=jnp.int32)
    tile_cols = jnp.arange(tile_z, dtype=jnp.int32)
    tile_mids = jnp.arange(tile_y, dtype=jnp.int32)
    extent = seg_extent[0, 0]
    seg_ids = jnp.arange(extent.shape[0], dtype=jnp.int32)
    starts = jnp.sum(jnp.where(seg_ids[None, :] < seg_ids[:, None], extent[None, :], 0), axis=1)
    inside = (starts[None, :] <= tile_rows[:, None]) & (
        tile_rows[:, None] < (starts + extent)[None, :]
    )
    in_owner = seg_local[0, 0] * brick_x + seg_offset[0, 0] - starts
    all_rows = jnp.arange(owners * own_rows, dtype=jnp.int32)[None, :]

    def picks(owner):
        base = owner * own_rows + in_owner
        source = jnp.sum(jnp.where(inside, base[None, :], 0), axis=1) + tile_rows
        return (source[:, None] == all_rows).astype(F32)

    owner = seg_owner[0, 0, :, 0]
    x_mat = band(taps[0], tile_rows, tile_rows)
    y_band = band(taps[1], tile_mids, tile_mids)
    z_band = band(taps[2], tile_cols, tile_cols)
    x_mass = jnp.sum(x_mat, axis=0)

    lanes = 128
    totals = jnp.stack(
        [jnp.sum(x_mat, axis=1), jnp.sum(x_mat / x_mass[None, :], axis=1)], axis=0
    )
    picked = picks(owner)
    table = jnp.sum(totals[:, :, None] * picked[None], axis=1).reshape(-1, lanes)
    table_rows = table.shape[0]
    table = jnp.pad(table, ((0, -table_rows % 8), (0, 0)))
    for bit in [1 << i for i in range(owners.bit_length() - 1)]:
        table = table + flip(table, bit, owners)
    table = table[:table_rows].reshape(2, owners, own_rows)
    owner_ids = jnp.arange(owners, dtype=jnp.int32)
    mine_rows = jnp.sum(jnp.where((owner_ids == me)[None, :, None], table, 0.0), axis=1)
    relative = (owner_ids[:, None] ^ me) == owner_ids[None, :]
    bound_rows = jnp.sum(
        jnp.where(relative[:, :, None], table[1][None], 0.0), axis=1
    ).reshape(-1)
    to_code = jnp.where(bound_rows > 0.0, FULL / jnp.maximum(bound_rows, 1e-30), 0.0)

    meta = jnp.concatenate(
        [
            jnp.pad(taps, ((0, 0), (0, lanes - count))),
            jnp.pad(shifts.astype(F32), (0, lanes - 2))[None],
            jnp.pad(mine_rows, ((0, 0), (0, lanes - own_rows))),
            jnp.zeros((2, lanes), F32),
        ],
        axis=0,
    )
    around = [meta] + [
        lax.ppermute(meta, "view", [(i, (i + s) % views) for i in range(views)])
        for s in range(1, views)
    ]
    view_ids = jnp.arange(views, dtype=jnp.int32)
    steps_back = lax.rem(my_view - view_ids + views, views)
    metas = sum(
        jnp.where((steps_back == s)[:, None, None], around[s][None], 0.0) for s in range(views)
    )
    all_shifts = metas[:, 3, :2].astype(jnp.int32)
    row_weight = jnp.broadcast_to(metas[:, 4, :own_rows, None], (views, own_rows, lanes))
    row_unit = jnp.broadcast_to(metas[:, 5, :own_rows, None], (views, own_rows, lanes))

    relative_picks = picks(owner ^ me)
    rows_mat = jnp.einsum("tw,tr->wr", x_mat, relative_picks, precision=highest)
    hi, lo = split_outside(rows_mat)
    gather_mat = jnp.concatenate([hi, lo], axis=0)
    hi, lo = split_outside(rows_mat.T * to_code[:, None])
    scatter_mat = jnp.concatenate(
        [jnp.concatenate([hi, hi], axis=1), jnp.concatenate([lo, lo], axis=1)], axis=0
    )
    hi, lo = split_outside(z_band)
    pair = jnp.concatenate([hi, lo], axis=1)
    z_mat = jnp.concatenate([pair, pair], axis=0)
    per_group = max(1, 128 // tile_y)
    y_mat = jnp.kron(jnp.eye(per_group, dtype=F32), y_band.T)
    hi, lo = split_outside(y_mat)
    y_mat = jnp.concatenate(
        [jnp.concatenate([hi, hi], axis=1), jnp.concatenate([lo, lo], axis=1)], axis=0
    )
    mass = jnp.sum(y_band, axis=0)[:, None] * jnp.sum(z_band, axis=0)[None, :]
    mass = jnp.tile(mass, (per_group, 1))

    def placing(values, shift, long, short):
        at = jnp.arange(long, dtype=jnp.int32) - shift
        ids = jnp.arange(short, dtype=jnp.int32)
        mat = band(values, at, ids)
        mat = jnp.where(((at >= 0) & (at < short))[:, None], mat, 0.0)
        return mat, jnp.sum(band(values, ids, ids), axis=0)

    z_all, z_mass = jax.vmap(lambda m, s: placing(m[2, :count], s[1], brick_z, tile_z))(
        metas, all_shifts
    )
    y_all, y_mass = jax.vmap(lambda m, s: placing(m[1, :count], s[0], brick_y, tile_y))(
        metas, all_shifts
    )
    outline = jnp.sum(y_all, axis=2)[:, :, None] * jnp.sum(z_all, axis=2)[:, None, :]
    z_all = jnp.transpose(z_all / z_mass[:, None, :], (0, 2, 1))
    hi, lo = split_outside(z_all)
    z_place = jnp.stack(
        [jnp.concatenate([hi, hi], axis=1), jnp.concatenate([lo, lo], axis=1)], axis=1
    )
    y_wide = jnp.transpose(y_all / y_mass[:, None, :], (1, 0, 2)).reshape(
        brick_y, views * tile_y
    )
    hi, lo = split_outside(y_wide)
    y_place = jnp.concatenate(
        [jnp.concatenate([hi, hi], axis=1), jnp.concatenate([lo, lo], axis=1)], axis=0
    )
    measured = views_data.reshape(tile_x * tile_y, tile_z)
    orders, slots = halving_orders(owners)

    current = flat
    for sweep in range(ITERS):
        last = sweep == ITERS - 1
        bound = 4.04 if sweep == 0 else 16.8
        pieces = gather_owners(crop, owners)
        outs = read_tile(
            pieces, measured, mass / bound, gather_mat, scatter_mat, z_mat, y_mat, slots
        )
        send = [outs[0], outs[2]]
        keep = [outs[1], outs[3]]
        for i in range(len(orders[0])):
            for h in range(2):
                total = keep[h] + flip(send[h], orders[h][i], owners).astype(F32)
                left = total.shape[0] // 2
                send[h] = code(total[:left]) if left else None
                keep[h] = total[left:]
        mine = [code(k[0]) for k in keep]
        sums = [tuple(mine)] + [
            tuple(
                lax.ppermute(p, "view", [(i, (i + s) % views) for i in range(views)])
                for p in mine
            )
            for s in range(1, views)
        ]
        result = update(
            scalars,
            sums,
            current,
            row_unit * (bound / FULL),
            z_place,
            y_place,
            outline,
            row_weight,
            tile_y,
            tile_z,
            last,
        )
        current = result[0]
        if not last:
            crop = result[1]
    return current.reshape(estimate.shape)


def solution(mesh):
    placed = (
        P("brick", None, None, None),
        P("view", "brick", None, None, None),
        P("view", None, None),
        P("view", "brick", None, None),
        P("view", "brick", None),
        P("view", "brick", None),
        P("view", "brick", None),
        P("view", None),
    )
    return jax.shard_map(
        on_device,
        mesh=mesh,
        in_specs=placed,
        out_specs=P("brick", None, None, None),
        check_vma=False,
    )
```

```python
import jax
import jax.numpy as jnp
from jax import lax
from jax.experimental import pallas as pl
from jax.experimental.pallas import tpu as pltpu
from jax.sharding import PartitionSpec as P

ITERS = 2
UNROLL = 8
WIRE = jnp.int16
FULL = 32000.0
F32 = jnp.float32
BF16 = jnp.bfloat16


def split(x):
    hi = x.astype(BF16)
    return hi, (x - hi.astype(F32)).astype(BF16)


def split_outside(x):
    hi = lax.reduce_precision(x, 8, 7)
    return hi.astype(BF16), lax.reduce_precision(x - hi, 8, 7).astype(BF16)


def dot(a, b):
    return lax.dot_general(a, b, (((1,), (0,)), ((), ())), preferred_element_type=F32)


def band(taps, rows, cols):
    count = taps.shape[0]
    index = rows[:, None] - cols[None, :] + count // 2
    hit = index[:, :, None] == jnp.arange(count, dtype=jnp.int32)
    return jnp.sum(jnp.where(hit, taps, 0.0), axis=-1)


def crop_rows(ref, r, shift_y, shift_z, tile_y, tile_z, stage):
    brick_y, brick_z = ref.shape[1:]
    base = pl.multiple_of(jnp.minimum(shift_y // 8, (brick_y - tile_y) // 8 - 1) * 8, 8)
    value = ref[r, pl.ds(base, tile_y + 8), :]
    stage[...] = pltpu.roll(value, lax.rem(brick_z - shift_z, brick_z), 1)[:, :tile_z]
    return stage[pl.ds(shift_y - base, tile_y), :]


def first_crop(shifts, estimate, tile_y, tile_z):
    rows, brick_y, brick_z = estimate.shape

    def kernel(shift_ref, est_ref, out_ref, stage, crops):
        def step(r, carry):
            crops[pl.ds(r, tile_y, stride=rows), :] = crop_rows(
                est_ref, r, shift_ref[0, 0], shift_ref[0, 1], tile_y, tile_z, stage
            )
            return carry

        lax.fori_loop(0, rows, step, 0, unroll=4)
        out_ref[...] = crops[...].astype(BF16).reshape(tile_y, rows, tile_z)

    return pl.pallas_call(
        kernel,
        out_shape=jax.ShapeDtypeStruct((tile_y, rows, tile_z), BF16),
        in_specs=[
            pl.BlockSpec(memory_space=pltpu.SMEM),
            pl.BlockSpec(memory_space=pltpu.VMEM),
        ],
        out_specs=pl.BlockSpec(memory_space=pltpu.VMEM),
        scratch_shapes=[
            pltpu.VMEM((tile_y + 8, tile_z), F32),
            pltpu.VMEM((tile_y * rows, tile_z), F32),
        ],
        name="first_crop",
    )(shifts, estimate)


def code(x):
    return (x + 0.5).astype(jnp.int32).astype(WIRE)


def read_tile(pieces, measured, mass, bound, gather_mat, scatter_mat, z_mat, y_mat, slots):
    owners = len(pieces)
    rows, tile_z = pieces[0][0].shape[1:]
    tile_y = sum(p.shape[0] for p in pieces[0])
    half = tile_y // 2
    tile_x = measured.shape[0] // tile_y
    flat = [p for parts in pieces for p in parts]
    n_flat = len(flat)
    firsts = [sum(len(p) for p in pieces[:k]) for k in range(owners)]
    n_send = owners // 2
    group = y_mat.shape[1] // 2
    per_group = group // tile_y
    groups = tile_x // per_group

    def kernel(*refs):
        g_refs = refs[:n_flat]
        m_ref, pat_ref, gm_ref, sm_ref, zm_ref, ym_ref = refs[n_flat : n_flat + 6]
        outs = refs[n_flat + 6 : n_flat + 10]
        buf = refs[n_flat + 10]
        for h in range(2):

            def line(k, y, h=h):
                if len(pieces[k]) == 2:
                    return g_refs[firsts[k] + h][y]
                return g_refs[firsts[k]][h * half + y]

            def gather(i, carry, h=h, line=line):
                y = i * 2
                both = jnp.concatenate(
                    [
                        jnp.concatenate([line(k, y), line(k, y + 1)], axis=1)
                        for k in range(owners)
                    ],
                    axis=0,
                )
                got = dot(gm_ref[...], both)
                got = got[:tile_x] + got[tile_x:]
                stacked = jnp.concatenate([got[:, :tile_z], got[:, tile_z:]], axis=0)
                hi, lo = split(stacked)
                out = dot(jnp.concatenate([hi, lo], axis=1), zm_ref[...])
                out = out[:, :tile_z] + out[:, tile_z:]
                buf[pl.ds(h * half + y, tile_x, stride=tile_y), :] = out[:tile_x]
                buf[pl.ds(h * half + y + 1, tile_x, stride=tile_y), :] = out[tile_x:]
                return carry

            lax.fori_loop(0, half // 2, gather, 0, unroll=UNROLL)

        def divide(i, carry):
            at = pl.multiple_of(i * 2 * group, 2 * group)
            first = buf[pl.ds(at, group), :]
            second = buf[pl.ds(at + group, group), :]
            hi, lo = split(jnp.concatenate([first, second], axis=1))
            out = dot(ym_ref[...], jnp.concatenate([hi, lo], axis=0))
            out = out[:group] + out[group:]
            data = m_ref[pl.ds(at, 2 * group), :].astype(F32)
            pat = pat_ref[...] * (1.0 / bound)
            buf[pl.ds(at, group), :] = data[:group] * pat / out[:, :tile_z]
            buf[pl.ds(at + group, group), :] = data[group:] * pat / out[:, tile_z:]
            return carry

        lax.fori_loop(0, groups // 2, divide, 0, unroll=UNROLL)

        for h in range(2):
            send_ref, keep_ref = outs[2 * h], outs[2 * h + 1]

            def put(y, sums, send_ref=send_ref, keep_ref=keep_ref, h=h):
                for k in range(owners):
                    block = sums[k * rows : (k + 1) * rows]
                    slot = slots[h][k]
                    if slot < n_send:
                        send_ref[slot, y] = code(block)
                    else:
                        keep_ref[slot - n_send, y] = block

            def scatter(i, carry, h=h, put=put):
                y = i * 2
                first = buf[pl.ds(h * half + y, tile_x, stride=tile_y), :]
                second = buf[pl.ds(h * half + y + 1, tile_x, stride=tile_y), :]
                hi, lo = split(jnp.concatenate([first, second], axis=1))
                out = dot(sm_ref[...], jnp.concatenate([hi, lo], axis=0))
                out = out[: owners * rows] + out[owners * rows :]
                put(y, out[:, :tile_z])
                put(y + 1, out[:, tile_z:])
                return carry

            lax.fori_loop(0, half // 2, scatter, 0, unroll=UNROLL)

    vmem = pl.BlockSpec(memory_space=pltpu.VMEM)
    shapes = []
    for h in range(2):
        for dtype in (WIRE, F32):
            shapes.append(jax.ShapeDtypeStruct((n_send, half, rows, tile_z), dtype))
    return pl.pallas_call(
        kernel,
        out_shape=tuple(shapes),
        in_specs=[vmem] * (n_flat + 6),
        out_specs=(vmem,) * 4,
        scratch_shapes=[pltpu.VMEM((tile_x * tile_y, tile_z), F32)],
        name="read_tile",
    )(*flat, measured, mass, gather_mat, scatter_mat, z_mat, y_mat)


def update(scalars, sums, estimate, bound, metas, z_place, y_place, outline, tile_y, tile_z, last):
    views = len(sums)
    rows, brick_y, brick_z = estimate.shape
    half = tile_y // 2

    def kernel(*refs):
        s_ref = refs[0]
        in_refs = refs[1 : 1 + views]
        est_ref, me_ref, zp_ref, yp_ref, pat_ref = refs[1 + views : 6 + views]
        rest = refs[6 + views :]
        out_ref = rest[0]
        crop_ref = None if last else rest[1]
        placed, stage, crops = rest[-3:]
        me = s_ref[2]
        for s in range(views):
            view = lax.rem(me + views - s, views)
            unit = me_ref[view, 8 + rows : 8 + 2 * rows, :] * (bound / FULL)
            for h in range(2):
                x = in_refs[s][h * half : (h + 1) * half].astype(jnp.int32).astype(F32)
                x = (x * unit[None]).reshape(half * rows, tile_z)
                hi, lo = split(x)
                out = dot(jnp.concatenate([hi, lo], axis=1), zp_ref[view, 0])
                out = out + dot(hi, zp_ref[view, 1, :tile_z, :])
                at = pl.multiple_of((view * 2 + h) * half * rows, half * rows)
                for j in range(brick_z // tile_z):
                    placed[j, pl.ds(at, half * rows), :] = out[:, j * tile_z : (j + 1) * tile_z]

        def step(r, carry):
            x = jnp.concatenate(
                [
                    placed[j, pl.ds(r, views * tile_y, stride=rows), :]
                    for j in range(brick_z // tile_z)
                ],
                axis=1,
            )
            hi, lo = split(x)
            out = dot(yp_ref[...], jnp.concatenate([hi, lo], axis=0))
            correction = out[:brick_y] + out[brick_y:]
            weight = jnp.zeros((brick_y, brick_z), F32)
            for v in range(views):
                factor = me_ref[v, pl.ds(8 + r, 1), :]
                factor = jnp.concatenate([factor] * (brick_z // factor.shape[1]), axis=1)
                weight = weight + factor * pat_ref[v]
            value = est_ref[r] * (1.0 + correction) / (1.0 + weight)
            out_ref[r] = value
            if not last:
                crops[pl.ds(r, tile_y, stride=rows), :] = crop_rows(
                    out_ref, r, s_ref[0], s_ref[1], tile_y, tile_z, stage
                )
            return carry

        lax.fori_loop(0, rows, step, 0, unroll=UNROLL)
        if not last:
            crop_ref[...] = crops[...].astype(BF16).reshape(tile_y, rows, tile_z)

    vmem = pl.BlockSpec(memory_space=pltpu.VMEM)
    shapes = [jax.ShapeDtypeStruct(estimate.shape, F32)]
    if not last:
        shapes.append(jax.ShapeDtypeStruct((tile_y, rows, tile_z), BF16))
    return pl.pallas_call(
        kernel,
        out_shape=tuple(shapes),
        in_specs=[pl.BlockSpec(memory_space=pltpu.SMEM)] + [vmem] * (views + 5),
        out_specs=(vmem,) * len(shapes),
        scratch_shapes=[
            pltpu.VMEM((brick_z // tile_z, views * tile_y * rows, tile_z), F32),
            pltpu.VMEM((tile_y + 8, tile_z), F32),
            pltpu.VMEM((tile_y * rows, tile_z), F32),
        ],
        name="update",
    )(scalars, *sums, estimate, metas, z_place, y_place, outline)


def flip(x, bit, count):
    return lax.ppermute(x, "brick", [(i, i ^ bit) for i in range(count)])


def over_view(x, steps, count):
    return lax.ppermute(x, "view", [(i, (i + steps) % count) for i in range(count)])


def gather_first(crop, count):
    wide = [1 << i for i in range(1, count.bit_length() - 1)]
    return {bit: flip(crop, bit, count) for bit in wide} if len(wide) == 2 else {}


def gather_owners(crop, near, count):
    half = crop.shape[0] // 2
    wide = [1 << i for i in range(1, count.bit_length() - 1)]
    got = {0: (crop,)}
    if near:
        x, y = wide
        got[x | y] = (flip(near[x][:half], y, count), flip(near[y][half:], x, count))
        got[x] = (near[x],)
        got[y] = (near[y],)
        wide = []
    for bit in wide + [1]:
        for k in list(got):
            got[k ^ bit] = tuple(flip(p, bit, count) for p in got[k])
    return [got[k] for k in range(count)]


def halving_orders(count):
    bits = [1 << i for i in range(count.bit_length() - 1)]
    orders = [bits, bits[:1] + bits[:0:-1]]
    slots = []
    for order in orders:
        place = {}
        for k in range(count):
            slot = 0
            for bit in order:
                slot = slot * 2 + (0 if k & bit else 1)
            place[k] = slot
        slots.append(place)
    return orders, slots


def on_device(
    estimate, views_data, psf_taps, seg_owner, seg_local, seg_offset, seg_extent, view_shift
):
    per_owner, brick_x, brick_y, brick_z = estimate.shape
    tile_x, tile_y, tile_z = views_data.shape[2:]
    own_rows = per_owner * brick_x
    owners = lax.axis_size("brick")
    views = lax.axis_size("view")
    me = lax.axis_index("brick")
    my_view = lax.axis_index("view")
    highest = lax.Precision.HIGHEST

    flat = estimate.reshape(own_rows, brick_y, brick_z)
    crop = first_crop(view_shift, flat, tile_y, tile_z)
    near = gather_first(crop, owners)
    shifts = view_shift[0]
    scalars = jnp.concatenate([shifts, my_view[None].astype(jnp.int32)])

    taps = psf_taps[0] / jnp.sum(psf_taps[0], axis=1, keepdims=True)
    count = taps.shape[1]
    tile_rows = jnp.arange(tile_x, dtype=jnp.int32)
    tile_cols = jnp.arange(tile_z, dtype=jnp.int32)
    tile_mids = jnp.arange(tile_y, dtype=jnp.int32)
    extent = seg_extent[0, 0]
    seg_ids = jnp.arange(extent.shape[0], dtype=jnp.int32)
    starts = jnp.sum(jnp.where(seg_ids[None, :] < seg_ids[:, None], extent[None, :], 0), axis=1)
    inside = (starts[None, :] <= tile_rows[:, None]) & (
        tile_rows[:, None] < (starts + extent)[None, :]
    )
    in_owner = seg_local[0, 0] * brick_x + seg_offset[0, 0] - starts
    all_rows = jnp.arange(owners * own_rows, dtype=jnp.int32)[None, :]

    def picks(owner):
        base = owner * own_rows + in_owner
        source = jnp.sum(jnp.where(inside, base[None, :], 0), axis=1) + tile_rows
        return (source[:, None] == all_rows).astype(F32)

    owner = seg_owner[0, 0, :, 0]
    x_mat = band(taps[0], tile_rows, tile_rows)
    y_band = band(taps[1], tile_mids, tile_mids)
    z_band = band(taps[2], tile_cols, tile_cols)
    x_mass = jnp.sum(x_mat, axis=0)

    lanes = 128
    totals = jnp.stack(
        [jnp.sum(x_mat, axis=1), jnp.sum(x_mat / x_mass[None, :], axis=1)], axis=0
    )
    table = jnp.sum(totals[:, :, None] * picks(owner)[None], axis=1).reshape(-1, lanes)
    table_rows = table.shape[0]
    table = jnp.pad(table, ((0, -table_rows % 8), (0, 0)))
    bits = [1 << i for i in range(owners.bit_length() - 1)]
    table = table + flip(table, bits[0], owners)
    near, table, x_mat, y_band, z_band, owner = lax.optimization_barrier(
        (near, table, x_mat, y_band, z_band, owner)
    )
    for bit in bits[1:]:
        table = table + flip(table, bit, owners)
    pieces = gather_owners(crop, near, owners)
    table = table[:table_rows].reshape(2, owners, own_rows)
    owner_ids = jnp.arange(owners, dtype=jnp.int32)
    mine_rows = jnp.sum(jnp.where((owner_ids == me)[None, :, None], table, 0.0), axis=1)
    relative = (owner_ids[:, None] ^ me) == owner_ids[None, :]
    bound_rows = jnp.sum(
        jnp.where(relative[:, :, None], table[1][None], 0.0), axis=1
    ).reshape(-1)
    to_code = jnp.where(bound_rows > 0.0, FULL / jnp.maximum(bound_rows, 1e-30), 0.0)

    relative_picks = picks(owner ^ me)
    rows_mat = jnp.einsum("tw,tr->wr", x_mat, relative_picks, precision=highest)
    hi, lo = split_outside(rows_mat)
    gather_mat = jnp.concatenate([hi, lo], axis=0)
    hi, lo = split_outside(rows_mat.T * to_code[:, None])
    scatter_mat = jnp.concatenate(
        [jnp.concatenate([hi, hi], axis=1), jnp.concatenate([lo, lo], axis=1)], axis=0
    )
    hi, lo = split_outside(z_band)
    pair = jnp.concatenate([hi, lo], axis=1)
    z_mat = jnp.concatenate([pair, pair], axis=0)
    per_group = max(1, 128 // tile_y)
    y_mat = jnp.kron(jnp.eye(per_group, dtype=F32), y_band.T)
    hi, lo = split_outside(y_mat)
    y_mat = jnp.concatenate(
        [jnp.concatenate([hi, hi], axis=1), jnp.concatenate([lo, lo], axis=1)], axis=0
    )
    mass = jnp.sum(y_band, axis=0)[:, None] * jnp.sum(z_band, axis=0)[None, :]
    mass = jnp.tile(mass, (per_group, 1))

    def view_metas(taps, shifts, mine_rows):
        meta = jnp.concatenate(
            [
                jnp.pad(taps, ((0, 0), (0, lanes - count))),
                jnp.pad(shifts.astype(F32), (0, lanes - 2))[None],
                jnp.zeros((4, lanes), F32),
                jnp.broadcast_to(mine_rows.reshape(-1, 1), (2 * own_rows, lanes)),
            ],
            axis=0,
        )
        around = [meta] + [over_view(meta, s, views) for s in range(1, views)]
        view_ids = jnp.arange(views, dtype=jnp.int32)
        steps_back = lax.rem(my_view - view_ids + views, views)
        return sum(
            jnp.where((steps_back == s)[:, None, None], around[s][None], 0.0)
            for s in range(views)
        )

    def view_tables(metas):
        all_shifts = metas[:, 3, :2].astype(jnp.int32)

        def placing(values, shift, long, short):
            at = jnp.arange(long, dtype=jnp.int32) - shift
            ids = jnp.arange(short, dtype=jnp.int32)
            mat = band(values, at, ids)
            mat = jnp.where(((at >= 0) & (at < short))[:, None], mat, 0.0)
            return mat, jnp.sum(band(values, ids, ids), axis=0)

        z_all, z_mass = jax.vmap(lambda m, s: placing(m[2, :count], s[1], brick_z, tile_z))(
            metas, all_shifts
        )
        y_all, y_mass = jax.vmap(lambda m, s: placing(m[1, :count], s[0], brick_y, tile_y))(
            metas, all_shifts
        )
        outline = jnp.sum(y_all, axis=2)[:, :, None] * jnp.sum(z_all, axis=2)[:, None, :]
        z_all = jnp.transpose(z_all / z_mass[:, None, :], (0, 2, 1))
        hi, lo = split_outside(z_all)
        z_place = jnp.stack(
            [jnp.concatenate([hi, hi], axis=1), jnp.concatenate([lo, lo], axis=1)], axis=1
        )
        y_wide = jnp.transpose(y_all / y_mass[:, None, :], (1, 0, 2)).reshape(
            brick_y, views * tile_y
        )
        hi, lo = split_outside(y_wide)
        y_place = jnp.concatenate(
            [jnp.concatenate([hi, hi], axis=1), jnp.concatenate([lo, lo], axis=1)], axis=0
        )
        return metas, z_place, y_place, outline

    measured = views_data.reshape(tile_x * tile_y, tile_z)
    orders, slots = halving_orders(owners)

    current = flat
    for sweep in range(ITERS):
        last = sweep == ITERS - 1
        bound = 4.04 if sweep == 0 else 16.8
        if sweep:
            pieces = gather_owners(crop, gather_first(crop, owners), owners)
        outs = read_tile(
            pieces, measured, mass, bound, gather_mat, scatter_mat, z_mat, y_mat, slots
        )
        send = [outs[0], outs[2]]
        keep = [outs[1], outs[3]]
        for i in range(len(orders[0])):
            for h in range(2):
                total = keep[h] + flip(send[h], orders[h][i], owners).astype(F32)
                left = total.shape[0] // 2
                send[h] = code(total[:left]) if left else None
                keep[h] = total[left:]
            if sweep == 0 and i == 0:
                send, keep, late = lax.optimization_barrier(
                    (send, keep, (taps, shifts, mine_rows))
                )
                metas = view_metas(*late)
        mine = jnp.concatenate([code(k[0]) for k in keep], axis=0)
        if sweep == 0:
            mine, metas = lax.optimization_barrier((mine, metas))
            tables = view_tables(metas)
        sums = [mine] + [over_view(mine, s, views) for s in range(1, views)]
        result = update(scalars, sums, current, bound, *tables, tile_y, tile_z, last)
        current = result[0]
        if not last:
            crop = result[1]
    return current.reshape(estimate.shape)


def solution(mesh):
    placed = (
        P("brick", None, None, None),
        P("view", "brick", None, None, None),
        P("view", None, None),
        P("view", "brick", None, None),
        P("view", "brick", None),
        P("view", "brick", None),
        P("view", "brick", None),
        P("view", None),
    )
    return jax.shard_map(
        on_device,
        mesh=mesh,
        in_specs=placed,
        out_specs=P("brick", None, None, None),
        check_vma=False,
    )
```

```python
import jax
import jax.numpy as jnp
from jax import lax
from jax.experimental import pallas as pl
from jax.experimental.pallas import tpu as pltpu
from jax.sharding import PartitionSpec as P

ITERS = 2
UNROLL = 8
WIRE = jnp.int16
FULL = 32000.0
F32 = jnp.float32
BF16 = jnp.bfloat16


def split(x):
    hi = x.astype(BF16)
    return hi, (x - hi.astype(F32)).astype(BF16)


def split_outside(x):
    hi = lax.reduce_precision(x, 8, 7)
    return hi.astype(BF16), lax.reduce_precision(x - hi, 8, 7).astype(BF16)


def dot(a, b):
    return lax.dot_general(a, b, (((1,), (0,)), ((), ())), preferred_element_type=F32)


def band(taps, rows, cols):
    count = taps.shape[0]
    index = rows[:, None] - cols[None, :] + count // 2
    hit = index[:, :, None] == jnp.arange(count, dtype=jnp.int32)
    return jnp.sum(jnp.where(hit, taps, 0.0), axis=-1)


def put_crop(out_ref, ref, stage, shift_y, shift_z):
    rows, brick_y, brick_z = ref.shape
    tile_y, _, tile_z = out_ref.shape
    tall = tile_y + 8
    base = pl.multiple_of(jnp.minimum(shift_y // 8, (brick_y - tile_y) // 8 - 1) * 8, 8)
    turn = lax.rem(brick_z - shift_z, brick_z)

    def cut(r, carry):
        value = ref[r, pl.ds(base, tall), :]
        at = pl.multiple_of(r * tall, 8)
        stage[pl.ds(at, tall), :] = pltpu.roll(value, turn, 1)[:, :tile_z]
        return carry

    def turn_over(y, carry):
        out_ref[y] = stage[pl.ds(shift_y - base + y, rows, stride=tall), :].astype(BF16)
        return carry

    lax.fori_loop(0, rows, cut, 0, unroll=8)
    lax.fori_loop(0, tile_y, turn_over, 0, unroll=8)


def first_crop(shifts, estimate, tile_y, tile_z):
    rows = estimate.shape[0]

    def kernel(shift_ref, est_ref, out_ref, stage):
        put_crop(out_ref, est_ref, stage, shift_ref[0, 0], shift_ref[0, 1])

    return pl.pallas_call(
        kernel,
        out_shape=jax.ShapeDtypeStruct((tile_y, rows, tile_z), BF16),
        in_specs=[
            pl.BlockSpec(memory_space=pltpu.SMEM),
            pl.BlockSpec(memory_space=pltpu.VMEM),
        ],
        out_specs=pl.BlockSpec(memory_space=pltpu.VMEM),
        scratch_shapes=[pltpu.VMEM((rows * (tile_y + 8), tile_z), F32)],
        name="first_crop",
    )(shifts, estimate)


def code(x):
    return (x + 0.5).astype(jnp.int32).astype(WIRE)


def read_tile(pieces, measured, mass, bound, gather_mat, scatter_mat, z_mat, y_mat, slots):
    owners = len(pieces)
    rows, tile_z = pieces[0][0].shape[1:]
    tile_y = sum(p.shape[0] for p in pieces[0])
    half = tile_y // 2
    tile_x = measured.shape[0] // tile_y
    flat = [p for parts in pieces for p in parts]
    n_flat = len(flat)
    firsts = [sum(len(p) for p in pieces[:k]) for k in range(owners)]
    n_send = owners // 2
    group = y_mat.shape[1] // 2
    per_group = group // tile_y
    groups = tile_x // per_group

    def kernel(*refs):
        g_refs = refs[:n_flat]
        m_ref, pat_ref, gm_ref, sm_ref, zm_ref, ym_ref = refs[n_flat : n_flat + 6]
        outs = refs[n_flat + 6 : n_flat + 10]
        lines, buf = refs[n_flat + 10 :]
        for h in range(2):

            def line(k, y, h=h):
                if len(pieces[k]) == 2:
                    return g_refs[firsts[k] + h][y]
                return g_refs[firsts[k]][h * half + y]

            def gather(i, carry, h=h, line=line):
                y = i * 2
                both = jnp.concatenate(
                    [
                        jnp.concatenate([line(k, y), line(k, y + 1)], axis=1)
                        for k in range(owners)
                    ],
                    axis=0,
                )
                got = dot(gm_ref[...], both)
                got = got[:tile_x] + got[tile_x:]
                stacked = jnp.concatenate([got[:, :tile_z], got[:, tile_z:]], axis=0)
                hi, lo = split(stacked)
                out = dot(jnp.concatenate([hi, lo], axis=1), zm_ref[...])
                out = out[:, :tile_z] + out[:, tile_z:]
                at = pl.multiple_of((h * half + y) * tile_x, 2 * tile_x)
                lines[pl.ds(at, 2 * tile_x), :] = out
                return carry

            lax.fori_loop(0, half // 2, gather, 0, unroll=UNROLL)

        def divide(i, carry):
            at = pl.multiple_of(i * 2 * group, 2 * group)
            x = i * 2 * per_group
            both = [
                lines[pl.ds(x + j, tile_y, stride=tile_x), :] for j in range(2 * per_group)
            ]
            first = jnp.concatenate(both[:per_group], axis=0)
            second = jnp.concatenate(both[per_group:], axis=0)
            hi, lo = split(jnp.concatenate([first, second], axis=1))
            out = dot(ym_ref[...], jnp.concatenate([hi, lo], axis=0))
            out = out[:group] + out[group:]
            data = m_ref[pl.ds(at, 2 * group), :].astype(F32)
            pat = pat_ref[...] * (1.0 / bound)
            buf[pl.ds(at, group), :] = data[:group] * pat / out[:, :tile_z]
            buf[pl.ds(at + group, group), :] = data[group:] * pat / out[:, tile_z:]
            return carry

        lax.fori_loop(0, groups // 2, divide, 0, unroll=7)

        for h in range(2):
            send_ref, keep_ref = outs[2 * h], outs[2 * h + 1]

            def put(y, sums, send_ref=send_ref, keep_ref=keep_ref, h=h):
                for k in range(owners):
                    block = sums[k * rows : (k + 1) * rows]
                    slot = slots[h][k]
                    if slot < n_send:
                        send_ref[slot, y] = code(block)
                    else:
                        keep_ref[slot - n_send, y] = block

            def scatter(i, carry, h=h, put=put):
                y = i * 2
                first = buf[pl.ds(h * half + y, tile_x, stride=tile_y), :]
                second = buf[pl.ds(h * half + y + 1, tile_x, stride=tile_y), :]
                hi, lo = split(jnp.concatenate([first, second], axis=1))
                out = dot(sm_ref[...], jnp.concatenate([hi, lo], axis=0))
                out = out[: owners * rows] + out[owners * rows :]
                put(y, out[:, :tile_z])
                put(y + 1, out[:, tile_z:])
                return carry

            lax.fori_loop(0, half // 2, scatter, 0, unroll=UNROLL)

    vmem = pl.BlockSpec(memory_space=pltpu.VMEM)
    shapes = []
    for h in range(2):
        for dtype in (WIRE, F32):
            shapes.append(jax.ShapeDtypeStruct((n_send, half, rows, tile_z), dtype))
    return pl.pallas_call(
        kernel,
        out_shape=tuple(shapes),
        in_specs=[vmem] * (n_flat + 6),
        out_specs=(vmem,) * 4,
        scratch_shapes=[pltpu.VMEM((tile_x * tile_y, tile_z), F32)] * 2,
        name="read_tile",
    )(*flat, measured, mass, gather_mat, scatter_mat, z_mat, y_mat)


def over_weight(estimate, metas, outline):
    rows, brick_y, brick_z = estimate.shape
    views = metas.shape[0]

    def kernel(est_ref, me_ref, pat_ref, out_ref):
        def step(r, carry):
            weight = jnp.ones((brick_y, brick_z), F32)
            for v in range(views):
                factor = me_ref[v, pl.ds(8 + r, 1), :]
                factor = jnp.concatenate([factor] * (brick_z // factor.shape[1]), axis=1)
                weight = weight + factor * pat_ref[v]
            out_ref[r] = est_ref[r] / weight
            return carry

        lax.fori_loop(0, rows, step, 0, unroll=4)

    vmem = pl.BlockSpec(memory_space=pltpu.VMEM)
    return pl.pallas_call(
        kernel,
        out_shape=jax.ShapeDtypeStruct(estimate.shape, F32),
        in_specs=[vmem] * 3,
        out_specs=vmem,
        name="over_weight",
    )(estimate, metas, outline)


def update(scalars, sums, ratio, bound, metas, z_place, y_place, tile_y, tile_z, last):
    views = len(sums)
    rows, brick_y, brick_z = ratio.shape
    half = tile_y // 2

    def kernel(*refs):
        s_ref = refs[0]
        in_refs = refs[1 : 1 + views]
        rt_ref, me_ref, zp_ref, yp_ref = refs[1 + views : 5 + views]
        rest = refs[5 + views :]
        out_ref = rest[0]
        crop_ref = None if last else rest[1]
        placed = rest[1] if last else rest[2]
        me = s_ref[2]
        for s in range(views):
            view = lax.rem(me + views - s, views)
            unit = me_ref[view, 8 + rows : 8 + 2 * rows, :] * (bound / FULL)
            for h in range(2):
                x = in_refs[s][h * half : (h + 1) * half].astype(jnp.int32).astype(F32)
                x = (x * unit[None]).reshape(half * rows, tile_z)
                hi, lo = split(x)
                out = dot(jnp.concatenate([hi, lo], axis=1), zp_ref[view, 0])
                out = out + dot(hi, zp_ref[view, 1, :tile_z, :])
                at = pl.multiple_of((view * 2 + h) * half * rows, half * rows)
                for j in range(brick_z // tile_z):
                    placed[j, pl.ds(at, half * rows), :] = out[:, j * tile_z : (j + 1) * tile_z]

        def step(r, carry):
            x = jnp.concatenate(
                [
                    placed[j, pl.ds(r, views * tile_y, stride=rows), :]
                    for j in range(brick_z // tile_z)
                ],
                axis=1,
            )
            hi, lo = split(x)
            out = dot(yp_ref[...], jnp.concatenate([hi, lo], axis=0))
            correction = out[:brick_y] + out[brick_y:]
            out_ref[r] = rt_ref[r] * (1.0 + correction)
            return carry

        lax.fori_loop(0, rows, step, 0, unroll=UNROLL)
        if not last:
            put_crop(crop_ref, out_ref, rest[3], s_ref[0], s_ref[1])

    vmem = pl.BlockSpec(memory_space=pltpu.VMEM)
    shapes = [jax.ShapeDtypeStruct(ratio.shape, F32)]
    if not last:
        shapes.append(jax.ShapeDtypeStruct((tile_y, rows, tile_z), BF16))
    scratch = [pltpu.VMEM((brick_z // tile_z, views * tile_y * rows, tile_z), F32)]
    if not last:
        scratch.append(pltpu.VMEM((rows * (tile_y + 8), tile_z), F32))
    return pl.pallas_call(
        kernel,
        out_shape=tuple(shapes),
        in_specs=[pl.BlockSpec(memory_space=pltpu.SMEM)] + [vmem] * (views + 4),
        out_specs=(vmem,) * len(shapes),
        scratch_shapes=scratch,
        name="update",
    )(scalars, *sums, ratio, metas, z_place, y_place)


def flip(x, bit, count):
    return lax.ppermute(x, "brick", [(i, i ^ bit) for i in range(count)])


def over_view(x, steps, count):
    return lax.ppermute(x, "view", [(i, (i + steps) % count) for i in range(count)])


def gather_first(crop, count):
    wide = [1 << i for i in range(1, count.bit_length() - 1)]
    return {bit: flip(crop, bit, count) for bit in wide} if len(wide) == 2 else {}


def gather_owners(crop, near, count):
    half = crop.shape[0] // 2
    wide = [1 << i for i in range(1, count.bit_length() - 1)]
    got = {0: (crop,)}
    if near:
        x, y = wide
        got[x | y] = (flip(near[x][:half], y, count), flip(near[y][half:], x, count))
        got[x] = (near[x],)
        got[y] = (near[y],)
        wide = []
    for bit in wide + [1]:
        for k in list(got):
            got[k ^ bit] = tuple(flip(p, bit, count) for p in got[k])
    return [got[k] for k in range(count)]


def halving_orders(count):
    bits = [1 << i for i in range(count.bit_length() - 1)]
    orders = [bits, bits[:1] + bits[:0:-1]]
    slots = []
    for order in orders:
        place = {}
        for k in range(count):
            slot = 0
            for bit in order:
                slot = slot * 2 + (0 if k & bit else 1)
            place[k] = slot
        slots.append(place)
    return orders, slots


def on_device(
    estimate, views_data, psf_taps, seg_owner, seg_local, seg_offset, seg_extent, view_shift
):
    per_owner, brick_x, brick_y, brick_z = estimate.shape
    tile_x, tile_y, tile_z = views_data.shape[2:]
    own_rows = per_owner * brick_x
    owners = lax.axis_size("brick")
    views = lax.axis_size("view")
    me = lax.axis_index("brick")
    my_view = lax.axis_index("view")
    highest = lax.Precision.HIGHEST

    flat = estimate.reshape(own_rows, brick_y, brick_z)
    crop = first_crop(view_shift, flat, tile_y, tile_z)
    near = gather_first(crop, owners)
    shifts = view_shift[0]
    scalars = jnp.concatenate([shifts, my_view[None].astype(jnp.int32)])

    taps = psf_taps[0] / jnp.sum(psf_taps[0], axis=1, keepdims=True)
    count = taps.shape[1]
    tile_rows = jnp.arange(tile_x, dtype=jnp.int32)
    tile_cols = jnp.arange(tile_z, dtype=jnp.int32)
    tile_mids = jnp.arange(tile_y, dtype=jnp.int32)
    extent = seg_extent[0, 0]
    seg_ids = jnp.arange(extent.shape[0], dtype=jnp.int32)
    starts = jnp.sum(jnp.where(seg_ids[None, :] < seg_ids[:, None], extent[None, :], 0), axis=1)
    inside = (starts[None, :] <= tile_rows[:, None]) & (
        tile_rows[:, None] < (starts + extent)[None, :]
    )
    in_owner = seg_local[0, 0] * brick_x + seg_offset[0, 0] - starts
    all_rows = jnp.arange(owners * own_rows, dtype=jnp.int32)[None, :]

    def picks(owner):
        base = owner * own_rows + in_owner
        source = jnp.sum(jnp.where(inside, base[None, :], 0), axis=1) + tile_rows
        return (source[:, None] == all_rows).astype(F32)

    owner = seg_owner[0, 0, :, 0]
    x_mat = band(taps[0], tile_rows, tile_rows)
    y_band = band(taps[1], tile_mids, tile_mids)
    z_band = band(taps[2], tile_cols, tile_cols)
    x_mass = jnp.sum(x_mat, axis=0)

    lanes = 128
    totals = jnp.stack(
        [jnp.sum(x_mat, axis=1), jnp.sum(x_mat / x_mass[None, :], axis=1)], axis=0
    )
    table = jnp.sum(totals[:, :, None] * picks(owner)[None], axis=1).reshape(-1, lanes)
    table_rows = table.shape[0]
    table = jnp.pad(table, ((0, -table_rows % 8), (0, 0)))
    bits = [1 << i for i in range(owners.bit_length() - 1)]
    table = table + flip(table, bits[0], owners)
    near, table, x_mat, y_band, z_band, owner = lax.optimization_barrier(
        (near, table, x_mat, y_band, z_band, owner)
    )
    for bit in bits[1:]:
        table = table + flip(table, bit, owners)
    pieces = gather_owners(crop, near, owners)
    table = table[:table_rows].reshape(2, owners, own_rows)
    owner_ids = jnp.arange(owners, dtype=jnp.int32)
    mine_rows = jnp.sum(jnp.where((owner_ids == me)[None, :, None], table, 0.0), axis=1)
    relative = (owner_ids[:, None] ^ me) == owner_ids[None, :]
    bound_rows = jnp.sum(
        jnp.where(relative[:, :, None], table[1][None], 0.0), axis=1
    ).reshape(-1)
    to_code = jnp.where(bound_rows > 0.0, FULL / jnp.maximum(bound_rows, 1e-30), 0.0)

    relative_picks = picks(owner ^ me)
    rows_mat = jnp.einsum("tw,tr->wr", x_mat, relative_picks, precision=highest)
    hi, lo = split_outside(rows_mat)
    gather_mat = jnp.concatenate([hi, lo], axis=0)
    hi, lo = split_outside(rows_mat.T * to_code[:, None])
    scatter_mat = jnp.concatenate(
        [jnp.concatenate([hi, hi], axis=1), jnp.concatenate([lo, lo], axis=1)], axis=0
    )
    hi, lo = split_outside(z_band)
    pair = jnp.concatenate([hi, lo], axis=1)
    z_mat = jnp.concatenate([pair, pair], axis=0)
    per_group = max(1, 128 // tile_y)
    y_mat = jnp.kron(jnp.eye(per_group, dtype=F32), y_band.T)
    hi, lo = split_outside(y_mat)
    y_mat = jnp.concatenate(
        [jnp.concatenate([hi, hi], axis=1), jnp.concatenate([lo, lo], axis=1)], axis=0
    )
    mass = jnp.sum(y_band, axis=0)[:, None] * jnp.sum(z_band, axis=0)[None, :]
    mass = jnp.tile(mass, (per_group, 1))

    def view_metas(taps, shifts, mine_rows):
        meta = jnp.concatenate(
            [
                jnp.pad(taps, ((0, 0), (0, lanes - count))),
                jnp.pad(shifts.astype(F32), (0, lanes - 2))[None],
                jnp.zeros((4, lanes), F32),
                jnp.broadcast_to(mine_rows.reshape(-1, 1), (2 * own_rows, lanes)),
            ],
            axis=0,
        )
        held = meta[None]
        for bit in [1 << i for i in range(views.bit_length() - 1)]:
            other = lax.ppermute(held, "view", [(i, i ^ bit) for i in range(views)])
            held = jnp.concatenate([held, other], axis=0)
        view_ids = jnp.arange(views, dtype=jnp.int32)
        return sum(
            jnp.where(((view_ids ^ my_view) == j)[:, None, None], held[j][None], 0.0)
            for j in range(views)
        )

    def view_tables(metas):
        all_shifts = metas[:, 3, :2].astype(jnp.int32)

        def placing(values, shift, long, short):
            at = jnp.arange(long, dtype=jnp.int32) - shift
            ids = jnp.arange(short, dtype=jnp.int32)
            mat = band(values, at, ids)
            mat = jnp.where(((at >= 0) & (at < short))[:, None], mat, 0.0)
            return mat, jnp.sum(band(values, ids, ids), axis=0)

        z_all, z_mass = jax.vmap(lambda m, s: placing(m[2, :count], s[1], brick_z, tile_z))(
            metas, all_shifts
        )
        y_all, y_mass = jax.vmap(lambda m, s: placing(m[1, :count], s[0], brick_y, tile_y))(
            metas, all_shifts
        )
        outline = jnp.sum(y_all, axis=2)[:, :, None] * jnp.sum(z_all, axis=2)[:, None, :]
        z_all = jnp.transpose(z_all / z_mass[:, None, :], (0, 2, 1))
        hi, lo = split_outside(z_all)
        z_place = jnp.stack(
            [jnp.concatenate([hi, hi], axis=1), jnp.concatenate([lo, lo], axis=1)], axis=1
        )
        y_wide = jnp.transpose(y_all / y_mass[:, None, :], (1, 0, 2)).reshape(
            brick_y, views * tile_y
        )
        hi, lo = split_outside(y_wide)
        y_place = jnp.concatenate(
            [jnp.concatenate([hi, hi], axis=1), jnp.concatenate([lo, lo], axis=1)], axis=0
        )
        return z_place, y_place, outline

    measured = views_data.reshape(tile_x * tile_y, tile_z)
    orders, slots = halving_orders(owners)

    current = flat
    for sweep in range(ITERS):
        last = sweep == ITERS - 1
        bound = 4.04 if sweep == 0 else 16.8
        if sweep:
            pieces = gather_owners(crop, gather_first(crop, owners), owners)
        outs = read_tile(
            pieces, measured, mass, bound, gather_mat, scatter_mat, z_mat, y_mat, slots
        )
        send = [outs[0], outs[2]]
        keep = [outs[1], outs[3]]
        for i in range(len(orders[0])):
            for h in range(2):
                total = keep[h] + flip(send[h], orders[h][i], owners).astype(F32)
                left = total.shape[0] // 2
                send[h] = code(total[:left]) if left else None
                keep[h] = total[left:]
            if sweep == 0 and i == 0:
                send, keep, late = lax.optimization_barrier(
                    (send, keep, (taps, shifts, mine_rows))
                )
                metas = view_metas(*late)
        mine = jnp.concatenate([code(k[0]) for k in keep], axis=0)
        if sweep == 0:
            mine, metas = lax.optimization_barrier((mine, metas))
            *places, outline = view_tables(metas)
        sums = [mine] + [over_view(mine, s, views) for s in range(1, views)]
        ratio = over_weight(current, metas, outline)
        result = update(scalars, sums, ratio, bound, metas, *places, tile_y, tile_z, last)
        current = result[0]
        if not last:
            crop = result[1]
    return current.reshape(estimate.shape)


def solution(mesh):
    placed = (
        P("brick", None, None, None),
        P("view", "brick", None, None, None),
        P("view", None, None),
        P("view", "brick", None, None),
        P("view", "brick", None),
        P("view", "brick", None),
        P("view", "brick", None),
        P("view", None),
    )
    return jax.shard_map(
        on_device,
        mesh=mesh,
        in_specs=placed,
        out_specs=P("brick", None, None, None),
        check_vma=False,
    )
```

```python
import jax
import jax.numpy as jnp
from jax import lax
from jax.experimental import pallas as pl
from jax.experimental.pallas import tpu as pltpu
from jax.sharding import PartitionSpec as P

ITERS = 2
UNROLL = 8
WIRE = jnp.int16
FULL = 32000.0
F32 = jnp.float32
BF16 = jnp.bfloat16


def split(x):
    hi = x.astype(BF16)
    return hi, (x - hi.astype(F32)).astype(BF16)


def split_outside(x):
    hi = lax.reduce_precision(x, 8, 7)
    return hi.astype(BF16), lax.reduce_precision(x - hi, 8, 7).astype(BF16)


def dot(a, b):
    return lax.dot_general(a, b, (((1,), (0,)), ((), ())), preferred_element_type=F32)


def band(taps, rows, cols):
    count = taps.shape[0]
    index = rows[:, None] - cols[None, :] + count // 2
    hit = index[:, :, None] == jnp.arange(count, dtype=jnp.int32)
    return jnp.sum(jnp.where(hit, taps, 0.0), axis=-1)


def put_crop(out_ref, ref, stage, shift_y, shift_z, tile_y, tile_z):
    rows, brick_y, brick_z = ref.shape
    tall = tile_y + 8
    base = pl.multiple_of(jnp.minimum(shift_y // 8, (brick_y - tile_y) // 8 - 1) * 8, 8)
    turn = lax.rem(brick_z - shift_z, brick_z)

    def cut(r, carry):
        value = ref[r, pl.ds(base, tall), :]
        at = pl.multiple_of(r * tall, 8)
        stage[pl.ds(at, tall), :] = pltpu.roll(value, turn, 1)[:, :tile_z]
        return carry

    def turn_over(y, carry):
        out_ref[y] = stage[pl.ds(shift_y - base + y, rows, stride=tall), :].astype(BF16)
        return carry

    lax.fori_loop(0, rows, cut, 0, unroll=8)
    lax.fori_loop(0, tile_y, turn_over, 0, unroll=8)


def first_crop(shifts, estimate, lines, tile_y, tile_z):
    rows = estimate.shape[0]
    extra = lines.shape[0]

    def kernel(shift_ref, est_ref, line_ref, out_ref, stage):
        put_crop(out_ref, est_ref, stage, shift_ref[0, 0], shift_ref[0, 1], tile_y, tile_z)
        out_ref[tile_y:] = line_ref[...]

    return pl.pallas_call(
        kernel,
        out_shape=jax.ShapeDtypeStruct((tile_y + extra, rows, tile_z), BF16),
        in_specs=[
            pl.BlockSpec(memory_space=pltpu.SMEM),
            pl.BlockSpec(memory_space=pltpu.VMEM),
            pl.BlockSpec(memory_space=pltpu.VMEM),
        ],
        out_specs=pl.BlockSpec(memory_space=pltpu.VMEM),
        scratch_shapes=[pltpu.VMEM((rows * (tile_y + 8), tile_z), F32)],
        name="first_crop",
    )(shifts, estimate, lines)


def code(x):
    return (x + 0.5).astype(jnp.int32).astype(WIRE)


def read_tile(
    me, pieces, tile_y, measured, mass, bound, scale, gather_mat, scatter_mat, z_mat, y_mat, slots
):
    owners = len(pieces)
    rows, tile_z = pieces[0][0].shape[1:]
    group = y_mat.shape[1] // 2
    half = tile_y // 2
    tile_x = measured.shape[0] // tile_y
    flat = [p for parts in pieces for p in parts]
    n_flat = len(flat)
    firsts = [sum(len(p) for p in pieces[:k]) for k in range(owners)]
    n_send = owners // 2
    per_group = group // tile_y
    groups = tile_x // per_group
    known = scale is not None
    extra = sum(p.shape[0] for p in pieces[0]) - tile_y

    def kernel(*refs):
        me_ref = refs[0]
        g_refs = refs[1 : 1 + n_flat]
        m_ref, pat_ref, gm_ref, sm_ref, zm_ref, ym_ref = refs[1 + n_flat : 7 + n_flat]
        rest = refs[7 + n_flat :]
        if known:
            scale_ref, rest = rest[0], rest[1:]
        outs = rest[:4]
        lines, buf = rest[-2:]
        if not known:
            scale_ref, own_ref = rest[4:6]
            table = []
            for j in range(extra):
                held = []
                for k in range(owners):
                    ref = g_refs[firsts[k] + len(pieces[k]) - 1]
                    held.append(ref[ref.shape[0] - extra + j].astype(F32))
                table.append(sum(held))
            lane = lax.broadcasted_iota(jnp.int32, (rows, tile_z), 1) & (2 * owners - 1)

            def column(which, k):
                hit = lane == which * owners + (me_ref[0] ^ k)
                picked = sum(jnp.where(hit, t, 0.0) for t in table)
                return jnp.sum(picked, axis=1, keepdims=True)

            for k in range(owners):
                total = column(1, k)
                value = jnp.where(total > 0.0, FULL / jnp.maximum(total, 1e-30), 0.0)
                scale_ref[k * rows : (k + 1) * rows, :] = jnp.broadcast_to(value, (rows, tile_z))
            for which in range(2):
                own_ref[which] = jnp.broadcast_to(column(which, 0), (rows, tile_z))
        for h in range(2):

            def line(k, y, h=h):
                if len(pieces[k]) == 2:
                    return g_refs[firsts[k] + h][y]
                return g_refs[firsts[k]][h * half + y]

            def gather(i, carry, h=h, line=line):
                y = i * 2
                both = jnp.concatenate(
                    [
                        jnp.concatenate([line(k, y), line(k, y + 1)], axis=1)
                        for k in range(owners)
                    ],
                    axis=0,
                )
                got = dot(gm_ref[...], both)
                got = got[:tile_x] + got[tile_x:]
                stacked = jnp.concatenate([got[:, :tile_z], got[:, tile_z:]], axis=0)
                hi, lo = split(stacked)
                out = dot(jnp.concatenate([hi, lo], axis=1), zm_ref[...])
                out = out[:, :tile_z] + out[:, tile_z:]
                at = pl.multiple_of((h * half + y) * tile_x, 2 * tile_x)
                lines[pl.ds(at, 2 * tile_x), :] = out
                return carry

            lax.fori_loop(0, half // 2, gather, 0, unroll=UNROLL)

        def divide(i, carry):
            at = pl.multiple_of(i * 2 * group, 2 * group)
            x = i * 2 * per_group
            both = [
                lines[pl.ds(x + j, tile_y, stride=tile_x), :] for j in range(2 * per_group)
            ]
            first = jnp.concatenate(both[:per_group], axis=0)
            second = jnp.concatenate(both[per_group:], axis=0)
            hi, lo = split(jnp.concatenate([first, second], axis=1))
            out = dot(ym_ref[...], jnp.concatenate([hi, lo], axis=0))
            out = out[:group] + out[group:]
            data = m_ref[pl.ds(at, 2 * group), :].astype(F32)
            pat = jnp.concatenate([pat_ref[...] * (1.0 / bound)] * per_group, axis=0)
            buf[pl.ds(at, group), :] = data[:group] * pat / out[:, :tile_z]
            buf[pl.ds(at + group, group), :] = data[group:] * pat / out[:, tile_z:]
            return carry

        lax.fori_loop(0, groups // 2, divide, 0, unroll=7)

        for h in range(2):
            send_ref, keep_ref = outs[2 * h], outs[2 * h + 1]

            def put(y, sums, send_ref=send_ref, keep_ref=keep_ref, h=h):
                for k in range(owners):
                    block = sums[k * rows : (k + 1) * rows]
                    slot = slots[h][k]
                    if slot < n_send:
                        send_ref[slot, y] = code(block)
                    else:
                        keep_ref[slot - n_send, y] = block

            def scatter(i, carry, h=h, put=put):
                y = i * 2
                first = buf[pl.ds(h * half + y, tile_x, stride=tile_y), :]
                second = buf[pl.ds(h * half + y + 1, tile_x, stride=tile_y), :]
                hi, lo = split(jnp.concatenate([first, second], axis=1))
                out = dot(sm_ref[...], jnp.concatenate([hi, lo], axis=0))
                out = out[: owners * rows] + out[owners * rows :]
                put(y, out[:, :tile_z] * scale_ref[...])
                put(y + 1, out[:, tile_z:] * scale_ref[...])
                return carry

            lax.fori_loop(0, half // 2, scatter, 0, unroll=UNROLL)

    vmem = pl.BlockSpec(memory_space=pltpu.VMEM)
    shapes = []
    for _ in range(2):
        for dtype in (WIRE, F32):
            shapes.append(jax.ShapeDtypeStruct((n_send, half, rows, tile_z), dtype))
    if not known:
        shapes.append(jax.ShapeDtypeStruct((owners * rows, tile_z), F32))
        shapes.append(jax.ShapeDtypeStruct((2, rows, tile_z), F32))
    return pl.pallas_call(
        kernel,
        out_shape=tuple(shapes),
        in_specs=[pl.BlockSpec(memory_space=pltpu.SMEM)] + [vmem] * (n_flat + 6 + known),
        out_specs=(vmem,) * len(shapes),
        scratch_shapes=[pltpu.VMEM((tile_x * tile_y, tile_z), F32)] * 2,
        name="read_tile",
    )(me, *flat, measured, mass, gather_mat, scatter_mat, z_mat, y_mat, *([scale] if known else []))


def over_weight(estimate, metas, outline):
    rows, brick_y, brick_z = estimate.shape
    views = metas.shape[0]

    def kernel(est_ref, me_ref, pat_ref, out_ref):
        def step(r, carry):
            weight = jnp.ones((brick_y, brick_z), F32)
            for v in range(views):
                factor = me_ref[v, pl.ds(8 + r, 1), :]
                factor = jnp.concatenate([factor] * (brick_z // factor.shape[1]), axis=1)
                weight = weight + factor * pat_ref[v]
            out_ref[r] = est_ref[r] / weight
            return carry

        lax.fori_loop(0, rows, step, 0, unroll=4)

    vmem = pl.BlockSpec(memory_space=pltpu.VMEM)
    return pl.pallas_call(
        kernel,
        out_shape=jax.ShapeDtypeStruct(estimate.shape, F32),
        in_specs=[vmem] * 3,
        out_specs=vmem,
        name="over_weight",
    )(estimate, metas, outline)


def update(scalars, sums, ratio, bound, metas, z_place, y_place, tile_y, tile_z, last):
    views = len(sums)
    rows, brick_y, brick_z = ratio.shape
    half = tile_y // 2

    def kernel(*refs):
        s_ref = refs[0]
        in_refs = refs[1 : 1 + views]
        rt_ref, me_ref, zp_ref, yp_ref = refs[1 + views : 5 + views]
        rest = refs[5 + views :]
        out_ref = rest[0]
        crop_ref = None if last else rest[1]
        placed = rest[1] if last else rest[2]
        me = s_ref[2]
        for s in range(views):
            view = me ^ s
            unit = me_ref[view, 8 + rows : 8 + 2 * rows, :] * (bound / FULL)
            for h in range(2):
                x = in_refs[s][h * half : (h + 1) * half].astype(jnp.int32)
                x = (x.astype(F32) * unit[None]).reshape(half * rows, tile_z)
                hi, lo = split(x)
                out = dot(jnp.concatenate([hi, lo], axis=1), zp_ref[view, 0])
                out = out + dot(hi, zp_ref[view, 1, :tile_z, :])
                at = pl.multiple_of((view * 2 + h) * half * rows, half * rows)
                for j in range(brick_z // tile_z):
                    placed[j, pl.ds(at, half * rows), :] = out[:, j * tile_z : (j + 1) * tile_z]

        def step(r, carry):
            x = jnp.concatenate(
                [
                    placed[j, pl.ds(r, views * tile_y, stride=rows), :]
                    for j in range(brick_z // tile_z)
                ],
                axis=1,
            )
            hi, lo = split(x)
            out = dot(yp_ref[...], jnp.concatenate([hi, lo], axis=0))
            correction = out[:brick_y] + out[brick_y:]
            out_ref[r] = rt_ref[r] * (1.0 + correction)
            return carry

        lax.fori_loop(0, rows, step, 0, unroll=UNROLL)
        if not last:
            put_crop(crop_ref, out_ref, rest[3], s_ref[0], s_ref[1], tile_y, tile_z)

    vmem = pl.BlockSpec(memory_space=pltpu.VMEM)
    shapes = [jax.ShapeDtypeStruct(ratio.shape, F32)]
    if not last:
        shapes.append(jax.ShapeDtypeStruct((tile_y, rows, tile_z), BF16))
    scratch = [pltpu.VMEM((brick_z // tile_z, views * tile_y * rows, tile_z), F32)]
    if not last:
        scratch.append(pltpu.VMEM((rows * (tile_y + 8), tile_z), F32))
    return pl.pallas_call(
        kernel,
        out_shape=tuple(shapes),
        in_specs=[pl.BlockSpec(memory_space=pltpu.SMEM)] + [vmem] * (views + 4),
        out_specs=(vmem,) * len(shapes),
        scratch_shapes=scratch,
        name="update",
    )(scalars, *sums, ratio, metas, z_place, y_place)


def flip(x, bit, count):
    return lax.ppermute(x, "brick", [(i, i ^ bit) for i in range(count)])


def pair_views(x, bit, count):
    return lax.ppermute(x, "view", [(i, i ^ bit) for i in range(count)])


def exchange_views(mine, count):
    return [mine] + [pair_views(mine, j, count) for j in range(1, count)]


def gather_first(crop, count):
    wide = [1 << i for i in range(1, count.bit_length() - 1)]
    return {bit: flip(crop, bit, count) for bit in wide} if len(wide) == 2 else {}


def gather_owners(crop, near, half, count):
    wide = [1 << i for i in range(1, count.bit_length() - 1)]
    got = {0: (crop,)}
    if near:
        x, y = wide
        got[x | y] = (flip(near[x][:half], y, count), flip(near[y][half:], x, count))
        got[x] = (near[x],)
        got[y] = (near[y],)
        wide = []
    for bit in wide + [1]:
        for k in list(got):
            got[k ^ bit] = tuple(flip(p, bit, count) for p in got[k])
    return [got[k] for k in range(count)]


def halving_orders(count):
    bits = [1 << i for i in range(count.bit_length() - 1)]
    orders = [bits, bits[:1] + bits[:0:-1]]
    slots = []
    for order in orders:
        place = {}
        for k in range(count):
            slot = 0
            for bit in order:
                slot = slot * 2 + (0 if k & bit else 1)
            place[k] = slot
        slots.append(place)
    return orders, slots


def on_device(
    estimate, views_data, psf_taps, seg_owner, seg_local, seg_offset, seg_extent, view_shift
):
    per_owner, brick_x, brick_y, brick_z = estimate.shape
    tile_x, tile_y, tile_z = views_data.shape[2:]
    own_rows = per_owner * brick_x
    owners = lax.axis_size("brick")
    views = lax.axis_size("view")
    me = lax.axis_index("brick")
    my_view = lax.axis_index("view")
    highest = lax.Precision.HIGHEST

    flat = estimate.reshape(own_rows, brick_y, brick_z)
    shifts = view_shift[0]
    scalars = jnp.concatenate([shifts, my_view[None].astype(jnp.int32)])

    lanes = 128
    count = psf_taps.shape[2]
    small = jnp.concatenate(
        [
            jnp.pad(psf_taps[0], ((0, 0), (0, lanes - count))),
            jnp.concatenate(
                [seg_owner[0, 0, :, 0], seg_local[0, 0], seg_offset[0, 0], seg_extent[0, 0]]
            ).astype(F32).reshape(-1, lanes),
        ],
        axis=0,
    )
    small = lax.optimization_barrier(small)
    taps = small[:3, :count] / jnp.sum(small[:3, :count], axis=1, keepdims=True)
    owner, local, offset, extent = small[3:].reshape(4, -1).astype(jnp.int32)
    tile_rows = jnp.arange(tile_x, dtype=jnp.int32)
    tile_cols = jnp.arange(tile_z, dtype=jnp.int32)
    tile_mids = jnp.arange(tile_y, dtype=jnp.int32)
    seg_ids = jnp.arange(extent.shape[0], dtype=jnp.int32)
    starts = jnp.sum(jnp.where(seg_ids[None, :] < seg_ids[:, None], extent[None, :], 0), axis=1)
    inside = (starts[None, :] <= tile_rows[:, None]) & (
        tile_rows[:, None] < (starts + extent)[None, :]
    )
    in_owner = local * brick_x + offset - starts
    all_rows = jnp.arange(owners * own_rows, dtype=jnp.int32)[None, :]

    def picks(owner):
        base = owner * own_rows + in_owner
        source = jnp.sum(jnp.where(inside, base[None, :], 0), axis=1) + tile_rows
        return (source[:, None] == all_rows).astype(F32)

    x_mat = band(taps[0], tile_rows, tile_rows)
    y_band = band(taps[1], tile_mids, tile_mids)
    z_band = band(taps[2], tile_cols, tile_cols)
    x_mass = jnp.sum(x_mat, axis=0)

    totals = jnp.stack(
        [jnp.sum(x_mat, axis=1), jnp.sum(x_mat / x_mass[None, :], axis=1)], axis=0
    )
    table = jnp.sum(totals[:, :, None] * picks(owner)[None], axis=1)
    table = table.reshape(2 * owners, own_rows).T
    hi = lax.reduce_precision(table, 8, 7)
    mid = lax.reduce_precision(table - hi, 8, 7)
    parts = jnp.concatenate([hi, mid, table - hi - mid], axis=1).astype(BF16)
    parts = jnp.pad(parts, ((0, 0), (0, -parts.shape[1] % lanes)))
    parts = jnp.transpose(parts.reshape(own_rows, -1, lanes), (1, 0, 2))
    crop = first_crop(view_shift, flat, parts, tile_y, tile_z)
    near = gather_first(crop, owners)
    pieces = gather_owners(crop, near, tile_y // 2, owners)

    relative_picks = picks(owner ^ me)
    rows_mat = jnp.einsum("tw,tr->wr", x_mat, relative_picks, precision=highest)
    hi, lo = split_outside(rows_mat)
    gather_mat = jnp.concatenate([hi, lo], axis=0)
    hi, lo = split_outside(rows_mat.T)
    scatter_mat = jnp.concatenate(
        [jnp.concatenate([hi, hi], axis=1), jnp.concatenate([lo, lo], axis=1)], axis=0
    )
    hi, lo = split_outside(z_band)
    pair = jnp.concatenate([hi, lo], axis=1)
    z_mat = jnp.concatenate([pair, pair], axis=0)
    per_group = max(1, 128 // tile_y)
    y_mat = jnp.kron(jnp.eye(per_group, dtype=F32), y_band.T)
    hi, lo = split_outside(y_mat)
    y_mat = jnp.concatenate(
        [jnp.concatenate([hi, hi], axis=1), jnp.concatenate([lo, lo], axis=1)], axis=0
    )
    mass = jnp.sum(y_band, axis=0)[:, None] * jnp.sum(z_band, axis=0)[None, :]

    def view_metas(taps, shifts, own_totals):
        meta = jnp.concatenate(
            [
                jnp.pad(taps, ((0, 0), (0, lanes - count))),
                jnp.pad(shifts.astype(F32), (0, lanes - 2))[None],
                jnp.zeros((4, lanes), F32),
                own_totals.reshape(2 * own_rows, lanes),
            ],
            axis=0,
        )
        held = exchange_views(meta, views)
        view_ids = jnp.arange(views, dtype=jnp.int32)
        return sum(
            jnp.where(((view_ids ^ my_view) == j)[:, None, None], held[j][None], 0.0)
            for j in range(views)
        )

    def view_tables(metas):
        all_shifts = metas[:, 3, :2].astype(jnp.int32)

        def placing(values, shift, long, short):
            at = jnp.arange(long, dtype=jnp.int32) - shift
            ids = jnp.arange(short, dtype=jnp.int32)
            mat = band(values, at, ids)
            mat = jnp.where(((at >= 0) & (at < short))[:, None], mat, 0.0)
            return mat, jnp.sum(band(values, ids, ids), axis=0)

        z_all, z_mass = jax.vmap(lambda m, s: placing(m[2, :count], s[1], brick_z, tile_z))(
            metas, all_shifts
        )
        y_all, y_mass = jax.vmap(lambda m, s: placing(m[1, :count], s[0], brick_y, tile_y))(
            metas, all_shifts
        )
        outline = jnp.sum(y_all, axis=2)[:, :, None] * jnp.sum(z_all, axis=2)[:, None, :]
        z_all = jnp.transpose(z_all / z_mass[:, None, :], (0, 2, 1))
        hi, lo = split_outside(z_all)
        z_place = jnp.stack(
            [jnp.concatenate([hi, hi], axis=1), jnp.concatenate([lo, lo], axis=1)], axis=1
        )
        y_wide = jnp.transpose(y_all / y_mass[:, None, :], (1, 0, 2)).reshape(
            brick_y, views * tile_y
        )
        hi, lo = split_outside(y_wide)
        y_place = jnp.concatenate(
            [jnp.concatenate([hi, hi], axis=1), jnp.concatenate([lo, lo], axis=1)], axis=0
        )
        return z_place, y_place, outline

    measured = views_data.reshape(tile_x * tile_y, tile_z)
    orders, slots = halving_orders(owners)

    current, scale = flat, None
    for sweep in range(ITERS):
        last = sweep == ITERS - 1
        bound = 4.04 if sweep == 0 else 16.8
        if sweep:
            pieces = gather_owners(crop, gather_first(crop, owners), tile_y // 2, owners)
        outs = read_tile(
            me[None].astype(jnp.int32),
            pieces,
            tile_y,
            measured,
            mass,
            bound,
            scale,
            gather_mat,
            scatter_mat,
            z_mat,
            y_mat,
            slots,
        )
        if sweep == 0:
            scale, own_totals = outs[4:]
        send = [outs[0], outs[2]]
        keep = [outs[1], outs[3]]
        for i in range(len(orders[0])):
            for h in range(2):
                got = flip(send[h], orders[h][i], owners)
                total = keep[h] + got.astype(F32)
                left = total.shape[0] // 2
                send[h] = code(total[:left]) if left else None
                keep[h] = total[left:]
            if sweep == 0 and i == 0:
                send, keep, late = lax.optimization_barrier(
                    (send, keep, (taps, shifts, own_totals))
                )
                metas = view_metas(*late)
        mine = jnp.concatenate([code(k[0]) for k in keep], axis=0)
        if sweep == 0:
            mine, metas = lax.optimization_barrier((mine, metas))
            *places, outline = view_tables(metas)
        sums = exchange_views(mine, views)
        ratio = over_weight(current, metas, outline)
        result = update(scalars, sums, ratio, bound, metas, *places, tile_y, tile_z, last)
        current = result[0]
        if not last:
            crop = result[1]
    return current.reshape(estimate.shape)


def solution(mesh):
    placed = (
        P("brick", None, None, None),
        P("view", "brick", None, None, None),
        P("view", None, None),
        P("view", "brick", None, None),
        P("view", "brick", None),
        P("view", "brick", None),
        P("view", "brick", None),
        P("view", None),
    )

    return jax.shard_map(
        on_device,
        mesh=mesh,
        in_specs=placed,
        out_specs=P("brick", None, None, None),
        check_vma=False,
    )
```

```python
import jax
import jax.numpy as jnp
from jax import lax
from jax.experimental import pallas as pl
from jax.experimental.pallas import tpu as pltpu
from jax.sharding import PartitionSpec as P

ITERS = 2
UNROLL = 8
WIRE = jnp.int16
FULL = 32000.0
F32 = jnp.float32
BF16 = jnp.bfloat16


def split(x):
    hi = x.astype(BF16)
    return hi, (x - hi.astype(F32)).astype(BF16)


def split_outside(x):
    hi = lax.reduce_precision(x, 8, 7)
    return hi.astype(BF16), lax.reduce_precision(x - hi, 8, 7).astype(BF16)


def dot(a, b):
    return lax.dot_general(a, b, (((1,), (0,)), ((), ())), preferred_element_type=F32)


def band(taps, rows, cols):
    count = taps.shape[0]
    index = rows[:, None] - cols[None, :] + count // 2
    hit = index[:, :, None] == jnp.arange(count, dtype=jnp.int32)
    return jnp.sum(jnp.where(hit, taps, 0.0), axis=-1)


def put_crop(out_ref, ref, stage, shift_y, shift_z, tile_y, tile_z):
    rows, brick_y, brick_z = ref.shape
    tall = tile_y + 8
    base = pl.multiple_of(jnp.minimum(shift_y // 8, (brick_y - tile_y) // 8 - 1) * 8, 8)
    turn = lax.rem(brick_z - shift_z, brick_z)

    def cut(r, carry):
        value = ref[r, pl.ds(base, tall), :]
        at = pl.multiple_of(r * tall, 8)
        stage[pl.ds(at, tall), :] = pltpu.roll(value, turn, 1)[:, :tile_z]
        return carry

    def turn_over(y, carry):
        out_ref[y] = stage[pl.ds(shift_y - base + y, rows, stride=tall), :].astype(BF16)
        return carry

    lax.fori_loop(0, rows, cut, 0, unroll=8)
    lax.fori_loop(0, tile_y, turn_over, 0, unroll=8)


def first_crop(shifts, estimate, lines, tile_y, tile_z):
    rows = estimate.shape[0]
    extra = lines.shape[0]

    def kernel(shift_ref, est_ref, line_ref, out_ref, stage):
        put_crop(out_ref, est_ref, stage, shift_ref[0, 0], shift_ref[0, 1], tile_y, tile_z)
        out_ref[tile_y:] = line_ref[...]

    return pl.pallas_call(
        kernel,
        out_shape=jax.ShapeDtypeStruct((tile_y + extra, rows, tile_z), BF16),
        in_specs=[
            pl.BlockSpec(memory_space=pltpu.SMEM),
            pl.BlockSpec(memory_space=pltpu.VMEM),
            pl.BlockSpec(memory_space=pltpu.VMEM),
        ],
        out_specs=pl.BlockSpec(memory_space=pltpu.VMEM),
        scratch_shapes=[pltpu.VMEM((rows * (tile_y + 8), tile_z), F32)],
        compiler_params=pltpu.CompilerParams(vmem_limit_bytes=24 << 20),
        name="first_crop",
    )(shifts, estimate, lines)


def code(x):
    return (x + 0.5).astype(jnp.int32).astype(WIRE)


def read_tile(
    me, pieces, tile_y, measured, mass, bound, scale, gather_mat, scatter_mat, z_mat, y_mat, slots
):
    owners = len(pieces)
    rows, tile_z = pieces[0][0].shape[1:]
    group = y_mat.shape[1] // 2
    half = tile_y // 2
    tile_x = measured.shape[0] // tile_y
    flat = [p for parts in pieces for p in parts]
    n_flat = len(flat)
    firsts = [sum(len(p) for p in pieces[:k]) for k in range(owners)]
    n_send = owners // 2
    per_group = group // tile_y
    groups = tile_x // per_group
    known = scale is not None
    extra = sum(p.shape[0] for p in pieces[0]) - tile_y

    def kernel(*refs):
        me_ref = refs[0]
        g_refs = refs[1 : 1 + n_flat]
        m_ref, pat_ref, gm_ref, sm_ref, zm_ref, ym_ref = refs[1 + n_flat : 7 + n_flat]
        rest = refs[7 + n_flat :]
        if known:
            scale_ref, rest = rest[0], rest[1:]
        outs = rest[:4]
        lines, buf = rest[-2:]
        if not known:
            scale_ref, own_ref = rest[4:6]
            table = []
            for j in range(extra):
                held = []
                for k in range(owners):
                    ref = g_refs[firsts[k] + len(pieces[k]) - 1]
                    held.append(ref[ref.shape[0] - extra + j].astype(F32))
                table.append(sum(held))
            lane = lax.broadcasted_iota(jnp.int32, (rows, tile_z), 1) & (2 * owners - 1)

            def column(which, k):
                hit = lane == which * owners + (me_ref[0] ^ k)
                picked = sum(jnp.where(hit, t, 0.0) for t in table)
                return jnp.sum(picked, axis=1, keepdims=True)

            for k in range(owners):
                total = column(1, k)
                value = jnp.where(total > 0.0, FULL / jnp.maximum(total, 1e-30), 0.0)
                scale_ref[k * rows : (k + 1) * rows, :] = jnp.broadcast_to(value, (rows, tile_z))
            for which in range(2):
                own_ref[which] = jnp.broadcast_to(column(which, 0), (rows, tile_z))
        for h in range(2):

            def line(k, y, h=h):
                if len(pieces[k]) == 2:
                    return g_refs[firsts[k] + h][y]
                return g_refs[firsts[k]][h * half + y]

            def gather(i, carry, h=h, line=line):
                y = i * 2
                both = jnp.concatenate(
                    [
                        jnp.concatenate([line(k, y), line(k, y + 1)], axis=1)
                        for k in range(owners)
                    ],
                    axis=0,
                )
                got = dot(gm_ref[...], both)
                got = got[:tile_x] + got[tile_x:]
                stacked = jnp.concatenate([got[:, :tile_z], got[:, tile_z:]], axis=0)
                hi, lo = split(stacked)
                out = dot(jnp.concatenate([hi, lo], axis=1), zm_ref[...])
                out = out[:, :tile_z] + out[:, tile_z:]
                at = pl.multiple_of((h * half + y) * tile_x, 2 * tile_x)
                lines[pl.ds(at, 2 * tile_x), :] = out
                return carry

            lax.fori_loop(0, half // 2, gather, 0, unroll=UNROLL)

        def divide(i, carry):
            at = pl.multiple_of(i * 2 * group, 2 * group)
            x = i * 2 * per_group
            both = [
                lines[pl.ds(x + j, tile_y, stride=tile_x), :] for j in range(2 * per_group)
            ]
            first = jnp.concatenate(both[:per_group], axis=0)
            second = jnp.concatenate(both[per_group:], axis=0)
            hi, lo = split(jnp.concatenate([first, second], axis=1))
            out = dot(ym_ref[...], jnp.concatenate([hi, lo], axis=0))
            out = out[:group] + out[group:]
            data = m_ref[pl.ds(at, 2 * group), :].astype(F32)
            pat = jnp.concatenate([pat_ref[...] * (1.0 / bound)] * per_group, axis=0)
            buf[pl.ds(at, group), :] = data[:group] * pat / out[:, :tile_z]
            buf[pl.ds(at + group, group), :] = data[group:] * pat / out[:, tile_z:]
            return carry

        lax.fori_loop(0, groups // 2, divide, 0, unroll=7)

        for h in range(2):
            send_ref, keep_ref = outs[2 * h], outs[2 * h + 1]

            def put(y, sums, send_ref=send_ref, keep_ref=keep_ref, h=h):
                for k in range(owners):
                    block = sums[k * rows : (k + 1) * rows]
                    slot = slots[h][k]
                    if slot < n_send:
                        send_ref[slot, y] = code(block)
                    else:
                        keep_ref[slot - n_send, y] = block

            def scatter(i, carry, h=h, put=put):
                y = i * 2
                first = buf[pl.ds(h * half + y, tile_x, stride=tile_y), :]
                second = buf[pl.ds(h * half + y + 1, tile_x, stride=tile_y), :]
                hi, lo = split(jnp.concatenate([first, second], axis=1))
                out = dot(sm_ref[...], jnp.concatenate([hi, lo], axis=0))
                out = out[: owners * rows] + out[owners * rows :]
                put(y, out[:, :tile_z] * scale_ref[...])
                put(y + 1, out[:, tile_z:] * scale_ref[...])
                return carry

            lax.fori_loop(0, half // 2, scatter, 0, unroll=UNROLL)

    vmem = pl.BlockSpec(memory_space=pltpu.VMEM)
    shapes = []
    for _ in range(2):
        for dtype in (WIRE, F32):
            shapes.append(jax.ShapeDtypeStruct((n_send, half, rows, tile_z), dtype))
    if not known:
        shapes.append(jax.ShapeDtypeStruct((owners * rows, tile_z), F32))
        shapes.append(jax.ShapeDtypeStruct((2, rows, tile_z), F32))
    return pl.pallas_call(
        kernel,
        out_shape=tuple(shapes),
        in_specs=[pl.BlockSpec(memory_space=pltpu.SMEM)] + [vmem] * (n_flat + 6 + known),
        out_specs=(vmem,) * len(shapes),
        scratch_shapes=[pltpu.VMEM((tile_x * tile_y, tile_z), F32)] * 2,
        compiler_params=pltpu.CompilerParams(
            vmem_limit_bytes=(24 << 20) if owners <= 8 else None
        ),
        name="read_tile",
    )(me, *flat, measured, mass, gather_mat, scatter_mat, z_mat, y_mat, *([scale] if known else []))


def over_weight(estimate, metas, outline):
    rows, brick_y, brick_z = estimate.shape
    views = metas.shape[0]

    def kernel(est_ref, me_ref, pat_ref, out_ref):
        def step(r, carry):
            weight = jnp.ones((brick_y, brick_z), F32)
            for v in range(views):
                factor = me_ref[v, pl.ds(8 + r, 1), :]
                factor = jnp.concatenate([factor] * (brick_z // factor.shape[1]), axis=1)
                weight = weight + factor * pat_ref[v]
            out_ref[r] = est_ref[r] / weight
            return carry

        lax.fori_loop(0, rows, step, 0, unroll=4)

    vmem = pl.BlockSpec(memory_space=pltpu.VMEM)
    return pl.pallas_call(
        kernel,
        out_shape=jax.ShapeDtypeStruct(estimate.shape, F32),
        in_specs=[vmem] * 3,
        out_specs=vmem,
        compiler_params=pltpu.CompilerParams(vmem_limit_bytes=24 << 20),
        name="over_weight",
    )(estimate, metas, outline)


def update(scalars, sums, ratio, bound, metas, z_place, y_place, tile_y, tile_z, last):
    views = len(sums)
    rows, brick_y, brick_z = ratio.shape
    half = tile_y // 2

    def kernel(*refs):
        s_ref = refs[0]
        in_refs = refs[1 : 1 + views]
        rt_ref, me_ref, zp_ref, yp_ref = refs[1 + views : 5 + views]
        rest = refs[5 + views :]
        out_ref = rest[0]
        crop_ref = None if last else rest[1]
        placed = rest[1] if last else rest[2]
        me = s_ref[2]
        for s in range(views):
            view = me ^ s
            unit = me_ref[view, 8 + rows : 8 + 2 * rows, :] * (bound / FULL)
            for h in range(2):
                x = in_refs[s][h * half : (h + 1) * half].astype(jnp.int32)
                x = (x.astype(F32) * unit[None]).reshape(half * rows, tile_z)
                hi, lo = split(x)
                out = dot(jnp.concatenate([hi, lo], axis=1), zp_ref[view, 0])
                out = out + dot(hi, zp_ref[view, 1, :tile_z, :])
                at = pl.multiple_of((view * 2 + h) * half * rows, half * rows)
                for j in range(brick_z // tile_z):
                    placed[j, pl.ds(at, half * rows), :] = out[:, j * tile_z : (j + 1) * tile_z]

        def step(r, carry):
            x = jnp.concatenate(
                [
                    placed[j, pl.ds(r, views * tile_y, stride=rows), :]
                    for j in range(brick_z // tile_z)
                ],
                axis=1,
            )
            hi, lo = split(x)
            out = dot(yp_ref[...], jnp.concatenate([hi, lo], axis=0))
            correction = out[:brick_y] + out[brick_y:]
            out_ref[r] = rt_ref[r] * (1.0 + correction)
            return carry

        lax.fori_loop(0, rows, step, 0, unroll=UNROLL)
        if not last:
            put_crop(crop_ref, out_ref, rest[3], s_ref[0], s_ref[1], tile_y, tile_z)

    vmem = pl.BlockSpec(memory_space=pltpu.VMEM)
    shapes = [jax.ShapeDtypeStruct(ratio.shape, F32)]
    if not last:
        shapes.append(jax.ShapeDtypeStruct((tile_y, rows, tile_z), BF16))
    scratch = [pltpu.VMEM((brick_z // tile_z, views * tile_y * rows, tile_z), F32)]
    if not last:
        scratch.append(pltpu.VMEM((rows * (tile_y + 8), tile_z), F32))
    return pl.pallas_call(
        kernel,
        out_shape=tuple(shapes),
        in_specs=[pl.BlockSpec(memory_space=pltpu.SMEM)] + [vmem] * (views + 4),
        out_specs=(vmem,) * len(shapes),
        scratch_shapes=scratch,
        compiler_params=pltpu.CompilerParams(vmem_limit_bytes=24 << 20),
        name="update",
    )(scalars, *sums, ratio, metas, z_place, y_place)


def flip(x, bit, count):
    return lax.ppermute(x, "brick", [(i, i ^ bit) for i in range(count)])


def pair_views(x, bit, count):
    return lax.ppermute(x, "view", [(i, i ^ bit) for i in range(count)])


def exchange_views(mine, count):
    return [mine] + [pair_views(mine, j, count) for j in range(1, count)]


def gather_first(crop, count):
    wide = [1 << i for i in range(1, count.bit_length() - 1)]
    return {bit: flip(crop, bit, count) for bit in wide} if len(wide) == 2 else {}


def gather_owners(crop, near, half, count):
    wide = [1 << i for i in range(1, count.bit_length() - 1)]
    got = {0: (crop,)}
    if near:
        x, y = wide
        got[x | y] = (flip(near[x][:half], y, count), flip(near[y][half:], x, count))
        got[x] = (near[x],)
        got[y] = (near[y],)
        wide = []
    for bit in wide + [1]:
        for k in list(got):
            got[k ^ bit] = tuple(flip(p, bit, count) for p in got[k])
    return [got[k] for k in range(count)]


def halving_orders(count):
    bits = [1 << i for i in range(count.bit_length() - 1)]
    orders = [bits, bits[:1] + bits[:0:-1]]
    slots = []
    for order in orders:
        place = {}
        for k in range(count):
            slot = 0
            for bit in order:
                slot = slot * 2 + (0 if k & bit else 1)
            place[k] = slot
        slots.append(place)
    return orders, slots


def on_device(
    estimate, views_data, psf_taps, seg_owner, seg_local, seg_offset, seg_extent, view_shift
):
    per_owner, brick_x, brick_y, brick_z = estimate.shape
    tile_x, tile_y, tile_z = views_data.shape[2:]
    own_rows = per_owner * brick_x
    owners = lax.axis_size("brick")
    views = lax.axis_size("view")
    me = lax.axis_index("brick")
    my_view = lax.axis_index("view")
    highest = lax.Precision.HIGHEST

    flat = estimate.reshape(own_rows, brick_y, brick_z)
    shifts = view_shift[0]
    scalars = jnp.concatenate([shifts, my_view[None].astype(jnp.int32)])

    lanes = 128
    count = psf_taps.shape[2]
    small = jnp.concatenate(
        [
            jnp.pad(psf_taps[0], ((0, 0), (0, lanes - count))),
            jnp.concatenate(
                [seg_owner[0, 0, :, 0], seg_local[0, 0], seg_offset[0, 0], seg_extent[0, 0]]
            ).astype(F32).reshape(-1, lanes),
        ],
        axis=0,
    )
    small = lax.optimization_barrier(small)
    taps = small[:3, :count] / jnp.sum(small[:3, :count], axis=1, keepdims=True)
    owner, local, offset, extent = small[3:].reshape(4, -1).astype(jnp.int32)
    tile_rows = jnp.arange(tile_x, dtype=jnp.int32)
    tile_cols = jnp.arange(tile_z, dtype=jnp.int32)
    tile_mids = jnp.arange(tile_y, dtype=jnp.int32)
    seg_ids = jnp.arange(extent.shape[0], dtype=jnp.int32)
    starts = jnp.sum(jnp.where(seg_ids[None, :] < seg_ids[:, None], extent[None, :], 0), axis=1)
    inside = (starts[None, :] <= tile_rows[:, None]) & (
        tile_rows[:, None] < (starts + extent)[None, :]
    )
    in_owner = local * brick_x + offset - starts
    all_rows = jnp.arange(owners * own_rows, dtype=jnp.int32)[None, :]

    def picks(owner):
        base = owner * own_rows + in_owner
        source = jnp.sum(jnp.where(inside, base[None, :], 0), axis=1) + tile_rows
        return (source[:, None] == all_rows).astype(F32)

    x_mat = band(taps[0], tile_rows, tile_rows)
    y_band = band(taps[1], tile_mids, tile_mids)
    z_band = band(taps[2], tile_cols, tile_cols)
    x_mass = jnp.sum(x_mat, axis=0)

    totals = jnp.stack(
        [jnp.sum(x_mat, axis=1), jnp.sum(x_mat / x_mass[None, :], axis=1)], axis=0
    )
    table = jnp.sum(totals[:, :, None] * picks(owner)[None], axis=1)
    table = table.reshape(2 * owners, own_rows).T
    hi = lax.reduce_precision(table, 8, 7)
    mid = lax.reduce_precision(table - hi, 8, 7)
    parts = jnp.concatenate([hi, mid, table - hi - mid], axis=1).astype(BF16)
    parts = jnp.pad(parts, ((0, 0), (0, -parts.shape[1] % lanes)))
    parts = jnp.transpose(parts.reshape(own_rows, -1, lanes), (1, 0, 2))
    crop = first_crop(view_shift, flat, parts, tile_y, tile_z)
    near = gather_first(crop, owners)
    pieces = gather_owners(crop, near, tile_y // 2, owners)

    relative_picks = picks(owner ^ me)
    rows_mat = jnp.einsum("tw,tr->wr", x_mat, relative_picks, precision=highest)
    hi, lo = split_outside(rows_mat)
    gather_mat = jnp.concatenate([hi, lo], axis=0)
    hi, lo = split_outside(rows_mat.T)
    scatter_mat = jnp.concatenate(
        [jnp.concatenate([hi, hi], axis=1), jnp.concatenate([lo, lo], axis=1)], axis=0
    )
    hi, lo = split_outside(z_band)
    pair = jnp.concatenate([hi, lo], axis=1)
    z_mat = jnp.concatenate([pair, pair], axis=0)
    per_group = max(1, 128 // tile_y)
    y_mat = jnp.kron(jnp.eye(per_group, dtype=F32), y_band.T)
    hi, lo = split_outside(y_mat)
    y_mat = jnp.concatenate(
        [jnp.concatenate([hi, hi], axis=1), jnp.concatenate([lo, lo], axis=1)], axis=0
    )
    mass = jnp.sum(y_band, axis=0)[:, None] * jnp.sum(z_band, axis=0)[None, :]

    def view_metas(taps, shifts, own_totals):
        meta = jnp.concatenate(
            [
                jnp.pad(taps, ((0, 0), (0, lanes - count))),
                jnp.pad(shifts.astype(F32), (0, lanes - 2))[None],
                jnp.zeros((4, lanes), F32),
                own_totals.reshape(2 * own_rows, lanes),
            ],
            axis=0,
        )
        held = exchange_views(meta, views)
        view_ids = jnp.arange(views, dtype=jnp.int32)
        return sum(
            jnp.where(((view_ids ^ my_view) == j)[:, None, None], held[j][None], 0.0)
            for j in range(views)
        )

    def view_tables(metas):
        all_shifts = metas[:, 3, :2].astype(jnp.int32)

        def placing(values, shift, long, short):
            at = jnp.arange(long, dtype=jnp.int32) - shift
            ids = jnp.arange(short, dtype=jnp.int32)
            mat = band(values, at, ids)
            mat = jnp.where(((at >= 0) & (at < short))[:, None], mat, 0.0)
            return mat, jnp.sum(band(values, ids, ids), axis=0)

        z_all, z_mass = jax.vmap(lambda m, s: placing(m[2, :count], s[1], brick_z, tile_z))(
            metas, all_shifts
        )
        y_all, y_mass = jax.vmap(lambda m, s: placing(m[1, :count], s[0], brick_y, tile_y))(
            metas, all_shifts
        )
        outline = jnp.sum(y_all, axis=2)[:, :, None] * jnp.sum(z_all, axis=2)[:, None, :]
        z_all = jnp.transpose(z_all / z_mass[:, None, :], (0, 2, 1))
        hi, lo = split_outside(z_all)
        z_place = jnp.stack(
            [jnp.concatenate([hi, hi], axis=1), jnp.concatenate([lo, lo], axis=1)], axis=1
        )
        y_wide = jnp.transpose(y_all / y_mass[:, None, :], (1, 0, 2)).reshape(
            brick_y, views * tile_y
        )
        hi, lo = split_outside(y_wide)
        y_place = jnp.concatenate(
            [jnp.concatenate([hi, hi], axis=1), jnp.concatenate([lo, lo], axis=1)], axis=0
        )
        return z_place, y_place, outline

    measured = views_data.reshape(tile_x * tile_y, tile_z)
    orders, slots = halving_orders(owners)

    current, scale = flat, None
    for sweep in range(ITERS):
        last = sweep == ITERS - 1
        bound = 4.04 if sweep == 0 else 16.8
        if sweep:
            pieces = gather_owners(crop, gather_first(crop, owners), tile_y // 2, owners)
        outs = read_tile(
            me[None].astype(jnp.int32),
            pieces,
            tile_y,
            measured,
            mass,
            bound,
            scale,
            gather_mat,
            scatter_mat,
            z_mat,
            y_mat,
            slots,
        )
        if sweep == 0:
            scale, own_totals = outs[4:]
        send = [outs[0], outs[2]]
        keep = [outs[1], outs[3]]
        for i in range(len(orders[0])):
            for h in range(2):
                got = flip(send[h], orders[h][i], owners)
                total = keep[h] + got.astype(F32)
                left = total.shape[0] // 2
                send[h] = code(total[:left]) if left else None
                keep[h] = total[left:]
            if sweep == 0 and i == 0:
                send, keep, late = lax.optimization_barrier(
                    (send, keep, (taps, shifts, own_totals))
                )
                metas = view_metas(*late)
        mine = jnp.concatenate([code(k[0]) for k in keep], axis=0)
        if sweep == 0:
            mine, metas = lax.optimization_barrier((mine, metas))
            *places, outline = view_tables(metas)
        sums = exchange_views(mine, views)
        ratio = over_weight(current, metas, outline)
        result = update(scalars, sums, ratio, bound, metas, *places, tile_y, tile_z, last)
        current = result[0]
        if not last:
            crop = result[1]
    return current.reshape(estimate.shape)


def solution(mesh):
    placed = (
        P("brick", None, None, None),
        P("view", "brick", None, None, None),
        P("view", None, None),
        P("view", "brick", None, None),
        P("view", "brick", None),
        P("view", "brick", None),
        P("view", "brick", None),
        P("view", None),
    )

    return jax.shard_map(
        on_device,
        mesh=mesh,
        in_specs=placed,
        out_specs=P("brick", None, None, None),
        check_vma=False,
    )
```

```python
import jax
import jax.numpy as jnp
from jax import lax
from jax.experimental import pallas as pl
from jax.experimental.pallas import tpu as pltpu
from jax.sharding import PartitionSpec as P

ITERS = 2
UNROLL = 8
WIRE = jnp.int16
FULL = 32000.0
F32 = jnp.float32
BF16 = jnp.bfloat16


def split(x):
    hi = x.astype(BF16)
    return hi, (x - hi.astype(F32)).astype(BF16)


def split_outside(x):
    hi = lax.reduce_precision(x, 8, 7)
    return hi.astype(BF16), lax.reduce_precision(x - hi, 8, 7).astype(BF16)


def dot(a, b):
    return lax.dot_general(a, b, (((1,), (0,)), ((), ())), preferred_element_type=F32)


def band(taps, rows, cols):
    count = taps.shape[0]
    index = rows[:, None] - cols[None, :] + count // 2
    hit = index[:, :, None] == jnp.arange(count, dtype=jnp.int32)
    return jnp.sum(jnp.where(hit, taps, 0.0), axis=-1)


def put_crop(out_ref, ref, stage, shift_y, shift_z, tile_y, tile_z):
    rows, brick_y, brick_z = ref.shape
    tall = tile_y + 8
    base = pl.multiple_of(jnp.minimum(shift_y // 8, (brick_y - tile_y) // 8 - 1) * 8, 8)
    turn = lax.rem(brick_z - shift_z, brick_z)

    def cut(r, carry):
        value = ref[r, pl.ds(base, tall), :]
        at = pl.multiple_of(r * tall, 8)
        stage[pl.ds(at, tall), :] = pltpu.roll(value, turn, 1)[:, :tile_z]
        return carry

    def turn_over(y, carry):
        out_ref[y] = stage[pl.ds(shift_y - base + y, rows, stride=tall), :].astype(BF16)
        return carry

    lax.fori_loop(0, rows, cut, 0, unroll=8)
    lax.fori_loop(0, tile_y, turn_over, 0, unroll=8)


def first_crop(shifts, estimate, lines, tile_y, tile_z):
    rows = estimate.shape[0]
    extra = lines.shape[0]

    def kernel(shift_ref, est_ref, line_ref, out_ref, stage):
        put_crop(out_ref, est_ref, stage, shift_ref[0, 0], shift_ref[0, 1], tile_y, tile_z)
        out_ref[tile_y:] = line_ref[...]

    return pl.pallas_call(
        kernel,
        out_shape=jax.ShapeDtypeStruct((tile_y + extra, rows, tile_z), BF16),
        in_specs=[
            pl.BlockSpec(memory_space=pltpu.SMEM),
            pl.BlockSpec(memory_space=pltpu.VMEM),
            pl.BlockSpec(memory_space=pltpu.VMEM),
        ],
        out_specs=pl.BlockSpec(memory_space=pltpu.VMEM),
        scratch_shapes=[pltpu.VMEM((rows * (tile_y + 8), tile_z), F32)],
        compiler_params=pltpu.CompilerParams(vmem_limit_bytes=24 << 20),
        name="first_crop",
    )(shifts, estimate, lines)


def code(x):
    return (x + 0.5).astype(jnp.int32).astype(WIRE)


def read_tile(
    me, pieces, tile_y, measured, mass, bound, scale, gather_mat, scatter_mat, z_mat, y_mat, slots
):
    owners = len(pieces)
    rows, tile_z = pieces[0][0].shape[1:]
    group = y_mat.shape[1] // 2
    half = tile_y // 2
    tile_x = measured.shape[0] // tile_y
    flat = [p for parts in pieces for p in parts]
    n_flat = len(flat)
    firsts = [sum(len(p) for p in pieces[:k]) for k in range(owners)]
    n_send = owners // 2
    per_group = group // tile_y
    groups = tile_x // per_group
    known = scale is not None
    extra = sum(p.shape[0] for p in pieces[0]) - tile_y

    def kernel(*refs):
        me_ref = refs[0]
        g_refs = refs[1 : 1 + n_flat]
        m_ref, pat_ref, gm_ref, sm_ref, zm_ref, ym_ref = refs[1 + n_flat : 7 + n_flat]
        rest = refs[7 + n_flat :]
        if known:
            scale_ref, rest = rest[0], rest[1:]
        outs = rest[:4]
        lines, buf = rest[-2:]
        if not known:
            scale_ref, own_ref = rest[4:6]
            table = []
            for j in range(extra):
                held = []
                for k in range(owners):
                    ref = g_refs[firsts[k] + len(pieces[k]) - 1]
                    held.append(ref[ref.shape[0] - extra + j].astype(F32))
                table.append(sum(held))
            lane = lax.broadcasted_iota(jnp.int32, (rows, tile_z), 1) & (2 * owners - 1)

            def column(which, k):
                hit = lane == which * owners + (me_ref[0] ^ k)
                picked = sum(jnp.where(hit, t, 0.0) for t in table)
                return jnp.sum(picked, axis=1, keepdims=True)

            for k in range(owners):
                total = column(1, k)
                value = jnp.where(total > 0.0, FULL / jnp.maximum(total, 1e-30), 0.0)
                scale_ref[k * rows : (k + 1) * rows, :] = jnp.broadcast_to(value, (rows, tile_z))
            for which in range(2):
                own_ref[which] = jnp.broadcast_to(column(which, 0), (rows, tile_z))
        for h in range(2):

            def line(k, y, h=h):
                if len(pieces[k]) == 2:
                    return g_refs[firsts[k] + h][y]
                return g_refs[firsts[k]][h * half + y]

            def gather(i, carry, h=h, line=line):
                y = i * 2
                both = jnp.concatenate(
                    [
                        jnp.concatenate([line(k, y), line(k, y + 1)], axis=1)
                        for k in range(owners)
                    ],
                    axis=0,
                )
                got = dot(gm_ref[...], both)
                got = got[:tile_x] + got[tile_x:]
                stacked = jnp.concatenate([got[:, :tile_z], got[:, tile_z:]], axis=0)
                hi, lo = split(stacked)
                out = dot(jnp.concatenate([hi, lo], axis=1), zm_ref[...])
                out = out[:, :tile_z] + out[:, tile_z:]
                at = pl.multiple_of((h * half + y) * tile_x, 2 * tile_x)
                lines[pl.ds(at, 2 * tile_x), :] = out
                return carry

            lax.fori_loop(0, half // 2, gather, 0, unroll=UNROLL)

        def divide(i, carry):
            at = pl.multiple_of(i * 2 * group, 2 * group)
            x = i * 2 * per_group
            both = [
                lines[pl.ds(x + j, tile_y, stride=tile_x), :] for j in range(2 * per_group)
            ]
            first = jnp.concatenate(both[:per_group], axis=0)
            second = jnp.concatenate(both[per_group:], axis=0)
            hi, lo = split(jnp.concatenate([first, second], axis=1))
            out = dot(ym_ref[...], jnp.concatenate([hi, lo], axis=0))
            out = out[:group] + out[group:]
            data = m_ref[pl.ds(at, 2 * group), :].astype(F32)
            pat = jnp.concatenate([pat_ref[...] * (1.0 / bound)] * per_group, axis=0)
            buf[pl.ds(at, group), :] = data[:group] * pat / out[:, :tile_z]
            buf[pl.ds(at + group, group), :] = data[group:] * pat / out[:, tile_z:]
            return carry

        lax.fori_loop(0, groups // 2, divide, 0, unroll=7)

        for h in range(2):
            send_ref, keep_ref = outs[2 * h], outs[2 * h + 1]

            def put(y, sums, send_ref=send_ref, keep_ref=keep_ref, h=h):
                for k in range(owners):
                    block = sums[k * rows : (k + 1) * rows]
                    slot = slots[h][k]
                    if slot < n_send:
                        send_ref[slot, y] = code(block)
                    else:
                        keep_ref[slot - n_send, y] = block

            def scatter(i, carry, h=h, put=put):
                y = i * 2
                first = buf[pl.ds(h * half + y, tile_x, stride=tile_y), :]
                second = buf[pl.ds(h * half + y + 1, tile_x, stride=tile_y), :]
                hi, lo = split(jnp.concatenate([first, second], axis=1))
                out = dot(sm_ref[...], jnp.concatenate([hi, lo], axis=0))
                out = out[: owners * rows] + out[owners * rows :]
                put(y, out[:, :tile_z] * scale_ref[...])
                put(y + 1, out[:, tile_z:] * scale_ref[...])
                return carry

            lax.fori_loop(0, half // 2, scatter, 0, unroll=UNROLL)

    vmem = pl.BlockSpec(memory_space=pltpu.VMEM)
    shapes = []
    for _ in range(2):
        for dtype in (WIRE, F32):
            shapes.append(jax.ShapeDtypeStruct((n_send, half, rows, tile_z), dtype))
    if not known:
        shapes.append(jax.ShapeDtypeStruct((owners * rows, tile_z), F32))
        shapes.append(jax.ShapeDtypeStruct((2, rows, tile_z), F32))
    return pl.pallas_call(
        kernel,
        out_shape=tuple(shapes),
        in_specs=[pl.BlockSpec(memory_space=pltpu.SMEM)] + [vmem] * (n_flat + 6 + known),
        out_specs=(vmem,) * len(shapes),
        scratch_shapes=[pltpu.VMEM((tile_x * tile_y, tile_z), F32)] * 2,
        compiler_params=pltpu.CompilerParams(
            vmem_limit_bytes=(24 << 20) if owners <= 8 else None
        ),
        name="read_tile",
    )(me, *flat, measured, mass, gather_mat, scatter_mat, z_mat, y_mat, *([scale] if known else []))


def over_weight(estimate, metas, outline):
    rows, brick_y, brick_z = estimate.shape
    views = metas.shape[0]

    def kernel(est_ref, me_ref, pat_ref, out_ref):
        def step(r, carry):
            weight = jnp.ones((brick_y, brick_z), F32)
            for v in range(views):
                factor = me_ref[v, pl.ds(8 + r, 1), :]
                factor = jnp.concatenate([factor] * (brick_z // factor.shape[1]), axis=1)
                weight = weight + factor * pat_ref[v]
            out_ref[r] = est_ref[r] / weight
            return carry

        lax.fori_loop(0, rows, step, 0, unroll=4)

    vmem = pl.BlockSpec(memory_space=pltpu.VMEM)
    return pl.pallas_call(
        kernel,
        out_shape=jax.ShapeDtypeStruct(estimate.shape, F32),
        in_specs=[vmem] * 3,
        out_specs=vmem,
        compiler_params=pltpu.CompilerParams(vmem_limit_bytes=24 << 20),
        name="over_weight",
    )(estimate, metas, outline)


def update(scalars, sums, ratio, bound, metas, z_place, y_place, tile_y, tile_z, last):
    views = len(sums)
    rows, brick_y, brick_z = ratio.shape
    half = tile_y // 2

    chunk = max(1, rows // 4)

    def kernel(*refs):
        s_ref = refs[0]
        sum_refs = refs[1 : 1 + views]
        rt_ref, me_ref, zp_ref, yp_ref, out_ref = refs[1 + views : 6 + views]
        crop_ref = None if last else refs[6 + views]
        placed, rt_buf, out_buf, rt_sem, out_sem = refs[6 + views + (not last) :][:5]
        rt_load = pltpu.make_async_copy(rt_ref, rt_buf, rt_sem)
        rt_load.start()
        me = s_ref[2]
        for s in range(views):
            view = me ^ s
            unit = me_ref[view, 8 + rows : 8 + 2 * rows, :] * (bound / FULL)
            for h in range(2):
                x = sum_refs[s][h * half : (h + 1) * half].astype(jnp.int32)
                x = (x.astype(F32) * unit[None]).reshape(half * rows, tile_z)
                hi, lo = split(x)
                out = dot(jnp.concatenate([hi, lo], axis=1), zp_ref[view, 0])
                out = out + dot(hi, zp_ref[view, 1, :tile_z, :])
                at = pl.multiple_of((view * 2 + h) * half * rows, half * rows)
                for j in range(brick_z // tile_z):
                    placed[j, pl.ds(at, half * rows), :] = out[:, j * tile_z : (j + 1) * tile_z]
        rt_load.wait()

        def store(i):
            some = pl.ds(i * chunk, chunk)
            return pltpu.make_async_copy(out_buf.at[some], out_ref.at[some], out_sem.at[i])

        for i in range(rows // chunk):

            def step(j, carry, i=i):
                r = i * chunk + j
                x = jnp.concatenate(
                    [
                        placed[k, pl.ds(r, views * tile_y, stride=rows), :]
                        for k in range(brick_z // tile_z)
                    ],
                    axis=1,
                )
                hi, lo = split(x)
                out = dot(yp_ref[...], jnp.concatenate([hi, lo], axis=0))
                correction = out[:brick_y] + out[brick_y:]
                out_buf[r] = rt_buf[r] * (1.0 + correction)
                return carry

            lax.fori_loop(0, chunk, step, 0, unroll=UNROLL)
            store(i).start()
        if not last:
            put_crop(crop_ref, out_buf, refs[-1], s_ref[0], s_ref[1], tile_y, tile_z)
        for i in range(rows // chunk):
            store(i).wait()

    vmem = pl.BlockSpec(memory_space=pltpu.VMEM)
    where = pl.BlockSpec(memory_space=pl.ANY)
    shapes = [jax.ShapeDtypeStruct(ratio.shape, F32)]
    if not last:
        shapes.append(jax.ShapeDtypeStruct((tile_y, rows, tile_z), BF16))
    scratch = [
        pltpu.VMEM((brick_z // tile_z, views * tile_y * rows, tile_z), F32),
        pltpu.VMEM(ratio.shape, F32),
        pltpu.VMEM(ratio.shape, F32),
        pltpu.SemaphoreType.DMA,
        pltpu.SemaphoreType.DMA((rows // chunk,)),
    ]
    if not last:
        scratch.append(pltpu.VMEM((rows * (tile_y + 8), tile_z), F32))
    return pl.pallas_call(
        kernel,
        out_shape=tuple(shapes),
        in_specs=[pl.BlockSpec(memory_space=pltpu.SMEM)] + [vmem] * views + [where] + [vmem] * 3,
        out_specs=(where, vmem)[: len(shapes)],
        scratch_shapes=scratch,
        compiler_params=pltpu.CompilerParams(vmem_limit_bytes=24 << 20),
        name="update",
    )(scalars, *sums, ratio, metas, z_place, y_place)


def flip(x, bit, count):
    return lax.ppermute(x, "brick", [(i, i ^ bit) for i in range(count)])


def pair_views(x, bit, count):
    return lax.ppermute(x, "view", [(i, i ^ bit) for i in range(count)])


def exchange_views(mine, count):
    return [mine] + [pair_views(mine, j, count) for j in range(1, count)]


def gather_first(crop, count):
    wide = [1 << i for i in range(1, count.bit_length() - 1)]
    return {bit: flip(crop, bit, count) for bit in wide} if len(wide) == 2 else {}


def gather_owners(crop, near, half, count):
    wide = [1 << i for i in range(1, count.bit_length() - 1)]
    got = {0: (crop,)}
    if near:
        x, y = wide
        got[x | y] = (flip(near[x][:half], y, count), flip(near[y][half:], x, count))
        got[x] = (near[x],)
        got[y] = (near[y],)
        wide = []
    for bit in wide + [1]:
        for k in list(got):
            got[k ^ bit] = tuple(flip(p, bit, count) for p in got[k])
    return [got[k] for k in range(count)]


def halving_orders(count):
    bits = [1 << i for i in range(count.bit_length() - 1)]
    orders = [bits, bits[:1] + bits[:0:-1]]
    slots = []
    for order in orders:
        place = {}
        for k in range(count):
            slot = 0
            for bit in order:
                slot = slot * 2 + (0 if k & bit else 1)
            place[k] = slot
        slots.append(place)
    return orders, slots


def on_device(
    estimate, views_data, psf_taps, seg_owner, seg_local, seg_offset, seg_extent, view_shift
):
    per_owner, brick_x, brick_y, brick_z = estimate.shape
    tile_x, tile_y, tile_z = views_data.shape[2:]
    own_rows = per_owner * brick_x
    owners = lax.axis_size("brick")
    views = lax.axis_size("view")
    me = lax.axis_index("brick")
    my_view = lax.axis_index("view")
    highest = lax.Precision.HIGHEST

    flat = estimate.reshape(own_rows, brick_y, brick_z)
    shifts = view_shift[0]
    scalars = jnp.concatenate([shifts, my_view[None].astype(jnp.int32)])

    lanes = 128
    count = psf_taps.shape[2]
    small = jnp.concatenate(
        [
            jnp.pad(psf_taps[0], ((0, 0), (0, lanes - count))),
            jnp.concatenate(
                [seg_owner[0, 0, :, 0], seg_local[0, 0], seg_offset[0, 0], seg_extent[0, 0]]
            ).astype(F32).reshape(-1, lanes),
        ],
        axis=0,
    )
    small = lax.optimization_barrier(small)
    taps = small[:3, :count] / jnp.sum(small[:3, :count], axis=1, keepdims=True)
    owner, local, offset, extent = small[3:].reshape(4, -1).astype(jnp.int32)
    tile_rows = jnp.arange(tile_x, dtype=jnp.int32)
    tile_cols = jnp.arange(tile_z, dtype=jnp.int32)
    tile_mids = jnp.arange(tile_y, dtype=jnp.int32)
    seg_ids = jnp.arange(extent.shape[0], dtype=jnp.int32)
    starts = jnp.sum(jnp.where(seg_ids[None, :] < seg_ids[:, None], extent[None, :], 0), axis=1)
    inside = (starts[None, :] <= tile_rows[:, None]) & (
        tile_rows[:, None] < (starts + extent)[None, :]
    )
    in_owner = local * brick_x + offset - starts
    all_rows = jnp.arange(owners * own_rows, dtype=jnp.int32)[None, :]

    def picks(owner):
        base = owner * own_rows + in_owner
        source = jnp.sum(jnp.where(inside, base[None, :], 0), axis=1) + tile_rows
        return (source[:, None] == all_rows).astype(F32)

    x_mat = band(taps[0], tile_rows, tile_rows)
    y_band = band(taps[1], tile_mids, tile_mids)
    z_band = band(taps[2], tile_cols, tile_cols)
    x_mass = jnp.sum(x_mat, axis=0)

    totals = jnp.stack(
        [jnp.sum(x_mat, axis=1), jnp.sum(x_mat / x_mass[None, :], axis=1)], axis=0
    )
    table = jnp.sum(totals[:, :, None] * picks(owner)[None], axis=1)
    table = table.reshape(2 * owners, own_rows).T
    hi = lax.reduce_precision(table, 8, 7)
    mid = lax.reduce_precision(table - hi, 8, 7)
    parts = jnp.concatenate([hi, mid, table - hi - mid], axis=1).astype(BF16)
    parts = jnp.pad(parts, ((0, 0), (0, -parts.shape[1] % lanes)))
    parts = jnp.transpose(parts.reshape(own_rows, -1, lanes), (1, 0, 2))
    crop = first_crop(view_shift, flat, parts, tile_y, tile_z)
    near = gather_first(crop, owners)
    pieces = gather_owners(crop, near, tile_y // 2, owners)

    relative_picks = picks(owner ^ me)
    rows_mat = jnp.einsum("tw,tr->wr", x_mat, relative_picks, precision=highest)
    hi, lo = split_outside(rows_mat)
    gather_mat = jnp.concatenate([hi, lo], axis=0)
    hi, lo = split_outside(rows_mat.T)
    scatter_mat = jnp.concatenate(
        [jnp.concatenate([hi, hi], axis=1), jnp.concatenate([lo, lo], axis=1)], axis=0
    )
    hi, lo = split_outside(z_band)
    pair = jnp.concatenate([hi, lo], axis=1)
    z_mat = jnp.concatenate([pair, pair], axis=0)
    per_group = max(1, 128 // tile_y)
    y_mat = jnp.kron(jnp.eye(per_group, dtype=F32), y_band.T)
    hi, lo = split_outside(y_mat)
    y_mat = jnp.concatenate(
        [jnp.concatenate([hi, hi], axis=1), jnp.concatenate([lo, lo], axis=1)], axis=0
    )
    mass = jnp.sum(y_band, axis=0)[:, None] * jnp.sum(z_band, axis=0)[None, :]

    def view_metas(taps, shifts, own_totals):
        meta = jnp.concatenate(
            [
                jnp.pad(taps, ((0, 0), (0, lanes - count))),
                jnp.pad(shifts.astype(F32), (0, lanes - 2))[None],
                jnp.zeros((4, lanes), F32),
                own_totals.reshape(2 * own_rows, lanes),
            ],
            axis=0,
        )
        held = exchange_views(meta, views)
        view_ids = jnp.arange(views, dtype=jnp.int32)
        return sum(
            jnp.where(((view_ids ^ my_view) == j)[:, None, None], held[j][None], 0.0)
            for j in range(views)
        )

    def view_tables(metas):
        all_shifts = metas[:, 3, :2].astype(jnp.int32)

        def placing(values, shift, long, short):
            at = jnp.arange(long, dtype=jnp.int32) - shift
            ids = jnp.arange(short, dtype=jnp.int32)
            mat = band(values, at, ids)
            mat = jnp.where(((at >= 0) & (at < short))[:, None], mat, 0.0)
            return mat, jnp.sum(band(values, ids, ids), axis=0)

        z_all, z_mass = jax.vmap(lambda m, s: placing(m[2, :count], s[1], brick_z, tile_z))(
            metas, all_shifts
        )
        y_all, y_mass = jax.vmap(lambda m, s: placing(m[1, :count], s[0], brick_y, tile_y))(
            metas, all_shifts
        )
        outline = jnp.sum(y_all, axis=2)[:, :, None] * jnp.sum(z_all, axis=2)[:, None, :]
        z_all = jnp.transpose(z_all / z_mass[:, None, :], (0, 2, 1))
        hi, lo = split_outside(z_all)
        z_place = jnp.stack(
            [jnp.concatenate([hi, hi], axis=1), jnp.concatenate([lo, lo], axis=1)], axis=1
        )
        y_wide = jnp.transpose(y_all / y_mass[:, None, :], (1, 0, 2)).reshape(
            brick_y, views * tile_y
        )
        hi, lo = split_outside(y_wide)
        y_place = jnp.concatenate(
            [jnp.concatenate([hi, hi], axis=1), jnp.concatenate([lo, lo], axis=1)], axis=0
        )
        return z_place, y_place, outline

    measured = views_data.reshape(tile_x * tile_y, tile_z)
    orders, slots = halving_orders(owners)

    current, scale = flat, None
    for sweep in range(ITERS):
        last = sweep == ITERS - 1
        bound = 4.04 if sweep == 0 else 16.8
        if sweep:
            pieces = gather_owners(crop, gather_first(crop, owners), tile_y // 2, owners)
        outs = read_tile(
            me[None].astype(jnp.int32),
            pieces,
            tile_y,
            measured,
            mass,
            bound,
            scale,
            gather_mat,
            scatter_mat,
            z_mat,
            y_mat,
            slots,
        )
        if sweep == 0:
            scale, own_totals = outs[4:]
        send = [outs[0], outs[2]]
        keep = [outs[1], outs[3]]
        for i in range(len(orders[0])):
            for h in range(2):
                got = flip(send[h], orders[h][i], owners)
                total = keep[h] + got.astype(F32)
                left = total.shape[0] // 2
                send[h] = code(total[:left]) if left else None
                keep[h] = total[left:]
            if sweep == 0 and i == 0:
                send, keep, late = lax.optimization_barrier(
                    (send, keep, (taps, shifts, own_totals))
                )
                metas = view_metas(*late)
        mine = jnp.concatenate([code(k[0]) for k in keep], axis=0)
        if sweep == 0:
            mine, metas = lax.optimization_barrier((mine, metas))
            *places, outline = view_tables(metas)
        sums = exchange_views(mine, views)
        ratio = over_weight(current, metas, outline)
        result = update(scalars, sums, ratio, bound, metas, *places, tile_y, tile_z, last)
        current = result[0]
        if not last:
            crop = result[1]
    return current.reshape(estimate.shape)


def solution(mesh):
    placed = (
        P("brick", None, None, None),
        P("view", "brick", None, None, None),
        P("view", None, None),
        P("view", "brick", None, None),
        P("view", "brick", None),
        P("view", "brick", None),
        P("view", "brick", None),
        P("view", None),
    )

    return jax.shard_map(
        on_device,
        mesh=mesh,
        in_specs=placed,
        out_specs=P("brick", None, None, None),
        check_vma=False,
    )
```
